128 devices in a mesh: seq: 8 (over z, core), tp: 16 (over x, y).
Axes of the slice: x: 4, y: 4, z: 4, core: 2. Of those that a mesh axis runs over, the one named last changes fastest.
Arguments:
- tokens: bfloat16 [2048, 6144], P(('seq', 'tp')), may hold values from -6 to 6
- proj_weight: bfloat16 [6144, 4, 4096], P(None, None, 'tp'), may hold values from -0.078125 to 0.078125
- out_weight: bfloat16 [4096, 6144], P('tp'), may hold values from -0.09375 to 0.09375
- head_gain: float32 [4096], P('tp'), may hold values from 0.1 to 1.9
- decay_rate: float32 [32], P('tp'), as said below
Outputs:
- layer_out: bfloat16 [2048, 6144], P(('seq', 'tp'))
The draws below stay inside these ranges and needn't reach their ends.
Inputs may be any that keep to these rules, and one draw needn't show every extreme that they name: `decay_rate`: every rate is positive.
All inputs are finite; a program needn't handle non-finite values.
Results may differ from the reference program's by a relative error of at most 0.015.
Values may be sent and summed in bfloat16 or wider, within the bound.
A program may use at most 128 MiB of HBM per device.

```python
import jax
import jax.numpy as jnp
from jax import lax

D = 6144
HEADS = 32
HD = 128
BLOCK = 256
TOKENS = 2048
N_TP = 16


def draw_decay_rate(key, part):
    key_mask, key_slow, key_fast = jax.random.split(key, 3)
    share = 0.5
    slow_heads = jax.random.uniform(key_mask, (HEADS,), jnp.float32) < share
    slow = jax.random.uniform(key_slow, (HEADS,), jnp.float32, 0.1, 2.0) / TOKENS
    fast = jnp.exp(jax.random.uniform(key_fast, (HEADS,), jnp.float32, jnp.log(1.0 / 500.0), jnp.log(1.0 / 30.0)))
    return jnp.where(slow_heads, slow, fast).astype(jnp.float32)


def shard_levels(key, dims, shards, least, high):
    def one(axis_at, shards_of):
        draws = jax.random.uniform(jax.random.fold_in(jax.random.fold_in(key, 6), axis_at), (shards_of,), jnp.float32, least / len(shards), high / len(shards))
        return jnp.repeat(jnp.exp(draws), dims[axis_at] // shards_of).reshape((-1,) + (1,) * (len(dims) - axis_at - 1))

    factor_of = one(*shards[0])
    for cut in shards[1:]:
        factor_of = factor_of * one(*cut)
    return factor_of


def normal_values(key, shape, spread, limit, shards=(), dtype=jnp.bfloat16):
    drawn = spread * jax.random.normal(key, shape, jnp.float32)
    if shards:
        drawn = drawn * shard_levels(key, shape, shards, -0.22, 0.18)
    return jnp.clip(drawn, -limit, limit).astype(dtype)


def setup_inputs(seed: int = 0) -> dict:
    key_list = jax.random.split(jax.random.key(seed), 6)
    return {
        "tokens": normal_values(key_list[0], (TOKENS, D), 1.0, 6.0, ((0, 128),)),
        "proj_weight": normal_values(key_list[1], (D, 4, HEADS * HD), D ** -0.5, 0.078125, ((2, 16),)),
        "out_weight": normal_values(key_list[2], (HEADS * HD, D), (HEADS * HD) ** -0.5, 0.09375, ((0, 16),)),
        "head_gain": jnp.clip(1.0 + 0.18 * jax.random.normal(key_list[3], (HEADS * HD,), jnp.float32), 0.1, 1.9),
        "decay_rate": draw_decay_rate(jax.random.fold_in(key_list[5], 71), 0),
    }


def attend(q_head, k_head, v_head, rate, start_state):
    count = q_head.shape[0] // BLOCK
    place = jnp.arange(BLOCK).astype(jnp.float32)
    diff = place[:, None] - place[None, :]
    causal = jnp.where(diff >= 0, jnp.exp(-rate * jnp.maximum(diff, 0.0)), 0.0)
    in_decay = jnp.exp(-rate * (place + 1.0))
    out_decay = jnp.exp(-rate * (BLOCK - 1.0 - place))
    block_decay = jnp.exp(-rate * BLOCK)
    q_blocks = q_head.reshape(count, BLOCK, q_head.shape[1])
    k_blocks = k_head.reshape(count, BLOCK, k_head.shape[1])
    v_blocks = v_head.reshape(count, BLOCK, v_head.shape[1])

    def advance(state, block):
        q_blk, k_blk, v_blk = block
        scores = jnp.dot(q_blk, k_blk.T, preferred_element_type=jnp.float32)
        weighted = (scores * causal).astype(jnp.bfloat16)
        inner = jnp.dot(weighted, v_blk, preferred_element_type=jnp.float32)
        carried = jnp.dot(q_blk.astype(jnp.float32), state, precision=lax.Precision.HIGHEST) * in_decay[:, None]
        scaled = k_blk.astype(jnp.float32) * out_decay[:, None]
        update = jnp.dot(scaled.T, v_blk.astype(jnp.float32), precision=lax.Precision.HIGHEST)
        return (block_decay * state + update, inner + carried)
    final_state, outputs = lax.scan(advance, start_state, (q_blocks, k_blocks, v_blocks))
    return (outputs.reshape(q_head.shape[0], q_head.shape[1]), final_state)

def finish(attn, gain, gate):
    square = lax.optimization_barrier(jnp.mean(attn * attn, axis=-1, keepdims=True))
    return attn * lax.rsqrt(square + 1e-06) * gain * jax.nn.sigmoid(gate)

def reference(tokens, proj_weight, out_weight, head_gain, decay_rate):

    def one_head(index):
        cols = lax.dynamic_slice_in_dim(proj_weight, index * HD, HD, 2).reshape(D, 4 * HD)
        mixed = jnp.dot(tokens, cols, preferred_element_type=jnp.float32)
        q_head = jax.nn.silu(mixed[:, :HD]).astype(jnp.bfloat16)
        k_head = jax.nn.silu(mixed[:, HD:2 * HD]).astype(jnp.bfloat16)
        v_head = jax.nn.silu(mixed[:, 2 * HD:3 * HD]).astype(jnp.bfloat16)
        rate = lax.dynamic_slice_in_dim(decay_rate, index, 1, 0)[0]
        gain = lax.dynamic_slice_in_dim(head_gain, index * HD, HD, 0)
        attn, unused = attend(q_head, k_head, v_head, rate, jnp.zeros((HD, HD), jnp.float32))
        return finish(attn, gain[None, :], mixed[:, 3 * HD:]).astype(jnp.bfloat16)
    heads_out = lax.map(one_head, jnp.arange(HEADS).astype(jnp.int32))
    joined = jnp.transpose(heads_out, (1, 0, 2)).reshape(TOKENS, HEADS * HD)
    group = HEADS * HD // N_TP

    def add_group(total, index):
        part_y = lax.dynamic_slice_in_dim(joined, index * group, group, 1)
        part_w = lax.dynamic_slice_in_dim(out_weight, index * group, group, 0)
        partial_sum = jnp.dot(part_y, part_w, preferred_element_type=jnp.float32).astype(jnp.bfloat16)
        partial_sum = lax.optimization_barrier(partial_sum)
        return (total + partial_sum.astype(jnp.float32), None)
    total, unused = lax.scan(add_group, jnp.zeros((TOKENS, D), jnp.float32), jnp.arange(N_TP).astype(jnp.int32))
    return total.astype(jnp.bfloat16)
```

```python
import jax
import jax.numpy as jnp
from jax import lax
from jax.experimental import pallas as pl
from jax.experimental.pallas import tpu as pltpu
from jax.sharding import PartitionSpec as P

HD = 128
ROWS = 16
BLOCK = 256
RING = 4
WCHUNKS = 6
BF = jnp.bfloat16
F32 = jnp.float32
MESH = pl.DeviceIdType.MESH


def fused(
    tok, w2h, woh, gain, rate, out,
    xga, xgb, w2, wf, wo, acc, mask, odec, idec, qb, kb, vb, ab, ybuf, pa, pb, rb,
    sloc, sbf, spart, tsend, tbuf, inc, isend, ibuf,
    ags, agr, rss, rsr, ws, misc, sts, str_,
):
    d = tok.shape[1]
    half = d // 2
    quart = half // 2
    seq = lax.axis_index("seq")
    tp = lax.axis_index("tp")
    z, core = seq // 2, lax.rem(seq, 2)
    x, y = tp // RING, lax.rem(tp, RING)

    def shift(v, s):
        return lax.rem(v + (s + RING), RING)

    near = {
        ("x", s): shift(x, s) * RING + y for s in (1, -1)
    } | {("y", s): x * RING + shift(y, s) for s in (1, -1)}
    prim, sec = ("x", "y"), ("y", "x")
    xg, part = (xga, xgb), (pa, pb)
    partner = z * 2 + (1 - core)

    def zpeer(dz):
        return lax.rem(z + dz, RING) * 2 + core

    barrier = pltpu.get_barrier_semaphore()
    for where in near.values():
        pl.semaphore_signal(barrier, inc=1, device_id={"tp": where}, device_id_type=MESH)
    for where in (partner, zpeer(1), zpeer(2), zpeer(3)):
        pl.semaphore_signal(barrier, inc=1, device_id={"seq": where}, device_id_type=MESH)

    wrows = w2.shape[0] // WCHUNKS
    loads = [
        pltpu.make_async_copy(
            w2h.at[pl.ds(c * wrows, wrows)], w2.at[pl.ds(c * wrows, wrows)], ws.at[c]
        )
        for c in range(WCHUNKS)
    ]
    loads[0].start()
    owns = [
        pltpu.make_async_copy(
            tok.at[:, pl.ds(h * half, half)], xg[h].at[pl.ds(0, ROWS)], misc.at[h]
        )
        for h in range(2)
    ]
    for c in owns:
        c.start()
    pl.semaphore_wait(barrier, 8)

    sent = []

    def push(src, dst, ssem, rsem, where):
        c = pltpu.make_async_remote_copy(
            src_ref=src, dst_ref=dst, send_sem=ssem, recv_sem=rsem,
            device_id=where, device_id_type=MESH,
        )
        c.start()
        sent.append(c)

    def spot(h, dp, dq, q):
        return xg[h].at[pl.ds((dq * RING + dp) * ROWS, ROWS), pl.ds(q * quart, quart)]

    def key(h, dp, dq, q):
        return h * 30 + (dq * RING + dp - 1) * 2 + q

    count = [0, 0]

    def gsend(h, dp, dq, q, along, s):
        if dp == 0 and dq == 0:
            src = tok.at[:, pl.ds(h * half + q * quart, quart)]
        else:
            src = spot(h, dp, dq, q)
        if along == 0:
            ndp, ndq, axis = (dp - s) % RING, dq, prim[h]
        else:
            ndp, ndq, axis = dp, (dq - s) % RING, sec[h]
        push(
            src, spot(h, ndp, ndq, q), ags.at[count[0]], agr.at[key(h, ndp, ndq, q)],
            {"tp": near[axis, s]},
        )
        count[0] += 1

    def gwait(h, dp, dq, q):
        pltpu.make_async_remote_copy(
            src_ref=spot(h, dp, dq, q), dst_ref=spot(h, dp, dq, q),
            send_sem=ags.at[0], recv_sem=agr.at[key(h, dp, dq, q)],
            device_id={"tp": near["x", 1]}, device_id_type=MESH,
        ).wait_recv()

    lead = {1: 0, -1: 1}
    for turn in range(2):
        for h in range(2):
            for s in (1, -1):
                gsend(h, 0, 0, lead[s] if turn == 0 else 1 - lead[s], 0, s)
    for turn in range(2):
        for h in range(2):
            for s in (1, -1):
                gsend(h, 0, 0, lead[s] if turn == 0 else 1 - lead[s], 1, s)
    for c in loads[1:]:
        c.start()
    wocopy = pltpu.make_async_copy(woh, wo, misc.at[2])
    wocopy.start()

    def place(dim, shape):
        i = lax.broadcasted_iota(jnp.int32, shape, dim)
        blk = i // ROWS
        dx, dy = blk & 3, blk // RING
        return (
            ((((x + dx) & 3) * RING + ((y + dy) & 3)) * ROWS + (i & (ROWS - 1)))
        ).astype(F32)

    diff = place(0, (BLOCK, BLOCK)) - place(1, (BLOCK, BLOCK))
    pos = place(0, (BLOCK, HD))
    for h in range(2):
        r = rate[h]
        mask[h] = jnp.where(diff >= 0.0, jnp.exp(-r * jnp.maximum(diff, 0.0)), 0.0)
        odec[h] = jnp.exp(-r * (BLOCK - 1.0 - pos))
        idec[h] = jnp.exp(-r * (pos + 1.0))
    acc[...] = jnp.zeros_like(acc)

    def reorder(c):
        loads[c].wait()
        each = wrows // 512

        def body(i, carry):
            for u in range(2):
                n = c * each + i * 2 + u
                v = w2[pl.ds(pl.multiple_of(n * 512, 512), 512), :].astype(F32)
                v = jnp.transpose(v.reshape(64, 8, 128), (1, 0, 2))
                r0 = pl.multiple_of(n * 64, 64)
                for e in range(8):
                    col = (e % 4) * 256 + (e // 4) * 128
                    wf[pl.ds(r0, 64), pl.ds(col, 128)] = v[e].astype(BF)
            return carry

        lax.fori_loop(0, each // 2, body, 0)

    def project(h, dq):
        def body(n, carry):
            cols = pl.ds(pl.multiple_of(n * 512, 512), 512)
            got = jnp.dot(
                xg[h][pl.ds(dq * 64, 64), :], wf[pl.ds(h * half, half), cols],
                preferred_element_type=F32,
            )
            if h == 0:
                acc[pl.ds(dq * 64, 64), cols] += got
            else:
                for dp in range(RING):
                    acc[pl.ds((dp * RING + dq) * ROWS, ROWS), cols] += got[dp * ROWS:(dp + 1) * ROWS]
            return carry

        lax.fori_loop(0, 2, body, 0)

    reorder(0)
    reorder(1)
    for h in range(2):
        for dp, q, s in ((3, 0, 1), (1, 1, -1)):
            gwait(h, dp, 0, q)
            gsend(h, dp, 0, q, 0, s)
            gsend(h, dp, 0, q, 1, 1)
            gsend(h, dp, 0, q, 1, -1)
    reorder(2)
    for h in range(2):
        for dq, q, s in ((3, 0, 1), (1, 1, -1)):
            gwait(h, 0, dq, q)
            gsend(h, 0, dq, q, 1, s)
        for dp, q in ((3, 1), (1, 0)):
            gwait(h, dp, 0, q)
            gsend(h, dp, 0, q, 1, 1)
            gsend(h, dp, 0, q, 1, -1)
    reorder(3)
    for h in range(2):
        for q in range(2):
            gwait(h, 2, 0, q)
            gsend(h, 2, 0, q, 1, 1)
            gsend(h, 2, 0, q, 1, -1)
    reorder(4)
    for dp in (3, 1):
        for h in range(2):
            for dq, q, s in ((3, 0, 1), (1, 1, -1)):
                gwait(h, dp, dq, q)
                gsend(h, dp, dq, q, 1, s)
    reorder(5)
    for h in range(2):
        for dq, q, s in ((3, 0, 1), (1, 1, -1)):
            gwait(h, 2, dq, q)
            gsend(h, 2, dq, q, 1, s)
    for c in owns:
        c.wait()
    for h in range(2):
        project(h, 0)
    for dq in (3, 1):
        for h in range(2):
            for dp in (0, 3, 1, 2):
                gwait(h, dp, dq, 1 if dq == 3 else 0)
            project(h, dq)
    for h in range(2):
        for dp in (0, 3, 1, 2):
            for q in range(2):
                gwait(h, dp, 2, q)
        project(h, 2)

    def silu(v):
        return v / (1.0 + jnp.exp(-v))

    kb[...] = silu(acc[:, 256:512]).astype(BF)
    vb[...] = silu(acc[:, 512:768]).astype(BF)
    for h in range(2):
        cols = pl.ds(h * HD, HD)
        ks = (kb[:, cols].astype(F32) * odec[h]).astype(BF)
        st = lax.dot_general(
            ks, vb[:, cols], (((0,), (0,)), ((), ())), preferred_element_type=F32
        )
        sloc[h] = st
        sbf[h] = st.astype(BF)

    def pair(src, dst, n, where):
        return pltpu.make_async_remote_copy(
            src_ref=src, dst_ref=dst, send_sem=sts.at[n], recv_sem=str_.at[n],
            device_id={"seq": where}, device_id_type=MESH,
        )

    swap = pair(sbf, spart, 0, partner)
    swap.start()
    qb[...] = silu(acc[:, 0:256]).astype(BF)

    def inner(h):
        cols = pl.ds(h * HD, HD)
        sc = lax.dot_general(
            qb[:, cols], kb[:, cols], (((1,), (1,)), ((), ())), preferred_element_type=F32
        )
        wt = (sc * mask[h]).astype(BF)
        ab[:, cols] = jnp.dot(wt, vb[:, cols], preferred_element_type=F32)

    def decay(r, n):
        return jnp.exp(jnp.full((1, HD), -r * n, F32))

    swap.wait()
    mine, other = sloc[core], spart[core].astype(F32)
    fall = decay(rate[core], float(BLOCK))
    first = core == 0
    one = jnp.ones_like(fall)
    chip = jnp.where(first, fall, one) * mine + jnp.where(first, one, fall) * other
    tsend[...] = chip.astype(BF)
    for dz in (1, 2, 3):
        @pl.when(z + dz < RING)
        def _(dz=dz):
            pair(tsend, tbuf.at[dz - 1], dz, zpeer(dz)).start()

    inner(0)
    inner(1)
    gate = 1.0 / (1.0 + jnp.exp(-acc[:, 768:1024]))
    acc[:, 768:1024] = gate * gain[...]
    inc[...] = jnp.zeros_like(inc)
    for dz in (1, 2, 3):
        @pl.when(z >= dz)
        def _(dz=dz):
            pair(tsend, tbuf.at[dz - 1], dz, zpeer(dz)).wait_recv()
            inc[...] += decay(rate[core], float(2 * BLOCK * (dz - 1))) * tbuf[dz - 1].astype(F32)

    isend[...] = inc[...].astype(BF)
    back = pair(isend, ibuf, 4, partner)
    back.start()
    back.wait()
    wocopy.wait()
    own_in, far_in = isend[...].astype(F32), ibuf[...].astype(F32)
    for h in range(2):
        cols = pl.ds(h * HD, HD)
        chipin = jnp.where(core == h, own_in, far_in)
        fallh = decay(rate[h], float(BLOCK))
        state = jnp.where(first, chipin, fallh * chipin + spart[h].astype(F32))
        carried = jnp.dot(qb[:, cols], state.astype(BF), preferred_element_type=F32)
        attn = ab[:, cols] + carried * idec[h]
        square = jnp.mean(attn * attn, axis=-1, keepdims=True)
        ybuf[:, cols] = (
            attn * lax.rsqrt(square + 1e-06) * acc[:, pl.ds(768 + h * HD, HD)]
        ).astype(BF)

    def blk(h, dp, dq):
        return (dq * RING + dp if h == 0 else dp * RING + dq) * ROWS

    def outproj(h, dq):
        if h == 0:
            rows = ybuf[pl.ds(dq * 64, 64), :]
        else:
            rows = jnp.concatenate([ybuf[pl.ds(blk(1, dp, dq), ROWS), :] for dp in range(RING)], axis=0)
        got = jnp.dot(rows, wo[:, pl.ds(h * half, half)], preferred_element_type=F32).astype(BF)
        for dp in range(RING):
            part[h][pl.ds(blk(h, dp, dq), ROWS), :] = got[dp * ROWS:(dp + 1) * ROWS]

    def piece(h, dp, dq, q):
        return part[h].at[pl.ds(blk(h, dp, dq), ROWS), pl.ds(q * quart, quart)]

    def rsend(h, dp, dq, q, n, along, s):
        axis = (prim if along == 0 else sec)[h]
        push(
            piece(h, dp, dq, q), rb.at[h * 30 + n], rss.at[count[1]], rsr.at[h * 30 + n],
            {"tp": near[axis, s]},
        )
        count[1] += 1

    def rwait(h, n):
        pltpu.make_async_remote_copy(
            src_ref=rb.at[h * 30 + n], dst_ref=rb.at[h * 30 + n],
            send_sem=rss.at[0], recv_sem=rsr.at[h * 30 + n],
            device_id={"tp": near["x", 1]}, device_id_type=MESH,
        ).wait_recv()
        return rb[h * 30 + n].astype(F32)

    def n_opp(dp, side):
        return dp * 2 + side

    def n_in(dp, side, q):
        return 8 + dp * 4 + side * 2 + q

    def opposite(h, dp):
        rsend(h, dp, 2, 0, n_opp(dp, 0), 1, 1)
        rsend(h, dp, 2, 1, n_opp(dp, 1), 1, -1)

    def direct(h, dp):
        rsend(h, dp, 1, 1, n_in(dp, 0, 1), 1, 1)
        rsend(h, dp, 3, 0, n_in(dp, 1, 0), 1, -1)

    def merged(h, dp):
        for dq, q, side, s in ((1, 0, 0, 1), (3, 1, 1, -1)):
            got = rwait(h, n_opp(dp, side))
            p = piece(h, dp, dq, q)
            p[...] = (p[...].astype(F32) + got).astype(BF)
            rsend(h, dp, dq, q, n_in(dp, side, q), 1, s)

    def gathered(h, dp, q):
        return (
            piece(h, dp, 0, q)[...].astype(F32)
            + rwait(h, n_in(dp, 0, q)) + rwait(h, n_in(dp, 1, q))
        )

    for h in range(2):
        outproj(h, 2)
    for h in range(2):
        opposite(h, 2)
    for h in range(2):
        outproj(h, 1)
        outproj(h, 3)
    for h in range(2):
        direct(h, 2)
        opposite(h, 1)
        opposite(h, 3)
    for h in range(2):
        outproj(h, 0)
    for h in range(2):
        merged(h, 2)
    for h in range(2):
        direct(h, 1)
        direct(h, 3)
        opposite(h, 0)
    for dp in (1, 3):
        for h in range(2):
            merged(h, dp)
    for h in range(2):
        for q, s in ((0, 1), (1, -1)):
            piece(h, 2, 0, q)[...] = gathered(h, 2, q).astype(BF)
            rsend(h, 2, 0, q, 24 + q, 0, s)
    for h in range(2):
        direct(h, 0)
    for h in range(2):
        merged(h, 0)
    for h in range(2):
        for dp, q, side, s in ((1, 1, 0, 1), (3, 0, 1, -1)):
            piece(h, dp, 0, q)[...] = gathered(h, dp, q).astype(BF)
            rsend(h, dp, 0, q, 26 + side * 2 + q, 0, s)
    for h in range(2):
        for dp, q, side, s in ((1, 0, 0, 1), (3, 1, 1, -1)):
            got = gathered(h, dp, q) + rwait(h, 24 + side)
            piece(h, dp, 0, q)[...] = got.astype(BF)
            rsend(h, dp, 0, q, 26 + side * 2 + q, 0, s)
    for h in range(2):
        for q in range(2):
            got = gathered(h, 0, q) + rwait(h, 26 + q) + rwait(h, 28 + q)
            out[:, pl.ds(h * half + q * quart, quart)] = got.astype(BF)

    for c in sent:
        c.wait_send()
    for dz in (1, 2, 3):
        @pl.when(z + dz < RING)
        def _(dz=dz):
            pair(tsend, tbuf.at[dz - 1], dz, zpeer(dz)).wait_send()


def per_device(tokens, proj_weight, out_weight, head_gain, decay_rate):
    d = tokens.shape[1]
    w2 = proj_weight.reshape(d, 4, 2, HD).transpose(0, 2, 1, 3).reshape(d * 8, HD)
    anyspace = pl.BlockSpec(memory_space=pl.ANY)
    vmem = pl.BlockSpec(memory_space=pltpu.VMEM)
    dma = pltpu.SemaphoreType.DMA
    v = pltpu.VMEM
    half = d // 2
    scratch = [
        v((BLOCK, half), BF), v((BLOCK, half), BF),
        v((d * 8, HD), BF), v((d, 1024), BF), v((256, d), BF),
        v((BLOCK, 1024), F32),
        v((2, BLOCK, BLOCK), F32), v((2, BLOCK, HD), F32), v((2, BLOCK, HD), F32),
        v((BLOCK, 256), BF), v((BLOCK, 256), BF), v((BLOCK, 256), BF),
        v((BLOCK, 256), F32), v((BLOCK, 256), BF),
        v((BLOCK, half), BF), v((BLOCK, half), BF),
        v((60, ROWS, half // 2), BF),
        v((2, HD, HD), F32), v((2, HD, HD), BF), v((2, HD, HD), BF),
        v((HD, HD), BF), v((3, HD, HD), BF), v((HD, HD), F32),
        v((HD, HD), BF), v((HD, HD), BF),
        dma((60,)), dma((60,)), dma((60,)), dma((60,)),
        dma((WCHUNKS,)), dma((3,)), dma((5,)), dma((5,)),
    ]
    return pl.pallas_call(
        fused,
        name="fused_layer",
        out_shape=jax.ShapeDtypeStruct(tokens.shape, BF),
        in_specs=[anyspace, anyspace, anyspace, vmem, pl.BlockSpec(memory_space=pltpu.SMEM)],
        out_specs=vmem,
        scratch_shapes=scratch,
        compiler_params=pltpu.CompilerParams(
            collective_id=0, has_side_effects=True, vmem_limit_bytes=60 * 1024 * 1024
        ),
    )(tokens, w2, out_weight, head_gain.reshape(1, -1), decay_rate)


def solution(mesh):
    return jax.shard_map(
        per_device,
        mesh=mesh,
        in_specs=(P(("seq", "tp"), None), P(None, None, "tp"), P("tp", None), P("tp"), P("tp")),
        out_specs=P(("seq", "tp"), None),
        check_vma=False,
    )
```

```python
import jax
import jax.numpy as jnp
from jax import lax
from jax.experimental import pallas as pl
from jax.experimental.pallas import tpu as pltpu
from jax.sharding import PartitionSpec as P

HD = 128
ROWS = 16
BLOCK = 256
RING = 4
WCHUNKS = 6
SLOT = (2, 0, 1, 3)
BF = jnp.bfloat16
F32 = jnp.float32
MESH = pl.DeviceIdType.MESH


def fused(
    tok, w2h, woh, gain, rate, out,
    xga, xgb, w2, wf, wo, acc, mask, odec, idec, qb, kb, vb, ab, ybuf, pa, pb, rb,
    sloc, sbf, spart, tsend, tbuf, inc, isend, ibuf,
    ags, agr, rss, rsr, ws, misc, sts, str_,
):
    d = tok.shape[1]
    half = d // 2
    quart = half // 2
    seq = lax.axis_index("seq")
    tp = lax.axis_index("tp")
    z, core = seq // 2, lax.rem(seq, 2)
    x, y = tp // RING, lax.rem(tp, RING)

    def shift(v, s):
        return lax.rem(v + (s + RING), RING)

    near = {
        ("x", s): shift(x, s) * RING + y for s in (1, -1)
    } | {("y", s): x * RING + shift(y, s) for s in (1, -1)}
    prim, sec = ("x", "y"), ("y", "x")
    xg, part = (xga, xgb), (pa, pb)
    partner = z * 2 + (1 - core)

    def zpeer(dz):
        return lax.rem(z + dz, RING) * 2 + core

    barrier = pltpu.get_barrier_semaphore()
    for where in near.values():
        pl.semaphore_signal(barrier, inc=1, device_id={"tp": where}, device_id_type=MESH)
    for where in (partner, zpeer(1), zpeer(2), zpeer(3)):
        pl.semaphore_signal(barrier, inc=1, device_id={"seq": where}, device_id_type=MESH)

    wrows = w2.shape[0] // WCHUNKS
    loads = [
        pltpu.make_async_copy(
            w2h.at[pl.ds(c * wrows, wrows)], w2.at[pl.ds(c * wrows, wrows)], ws.at[c]
        )
        for c in range(WCHUNKS)
    ]
    loads[0].start()
    owns = [
        pltpu.make_async_copy(
            tok.at[:, pl.ds(h * half, half)], xg[h].at[pl.ds(0, ROWS)], misc.at[h]
        )
        for h in range(2)
    ]
    for c in owns:
        c.start()
    pl.semaphore_wait(barrier, 8)

    sent = []

    def push(src, dst, ssem, rsem, where):
        c = pltpu.make_async_remote_copy(
            src_ref=src, dst_ref=dst, send_sem=ssem, recv_sem=rsem,
            device_id=where, device_id_type=MESH,
        )
        c.start()
        sent.append(c)

    def spot(h, dp, dq, q):
        return xg[h].at[pl.ds((dq * RING + dp) * ROWS, ROWS), pl.ds(q * quart, quart)]

    def key(h, dp, dq, q):
        return h * 30 + (dq * RING + dp - 1) * 2 + q

    count = [0, 0]

    def gsend(h, dp, dq, q, along, s):
        if dp == 0 and dq == 0:
            src = tok.at[:, pl.ds(h * half + q * quart, quart)]
        else:
            src = spot(h, dp, dq, q)
        if along == 0:
            ndp, ndq, axis = (dp - s) % RING, dq, prim[h]
        else:
            ndp, ndq, axis = dp, (dq - s) % RING, sec[h]
        push(
            src, spot(h, ndp, ndq, q), ags.at[count[0]], agr.at[key(h, ndp, ndq, q)],
            {"tp": near[axis, s]},
        )
        count[0] += 1

    def gwait(h, dp, dq, q):
        pltpu.make_async_remote_copy(
            src_ref=spot(h, dp, dq, q), dst_ref=spot(h, dp, dq, q),
            send_sem=ags.at[0], recv_sem=agr.at[key(h, dp, dq, q)],
            device_id={"tp": near["x", 1]}, device_id_type=MESH,
        ).wait_recv()

    lead = {1: 0, -1: 1}
    for turn in range(2):
        for h in range(2):
            for s in (1, -1):
                gsend(h, 0, 0, lead[s] if turn == 0 else 1 - lead[s], 0, s)
    for turn in range(2):
        for h in range(2):
            for s in (1, -1):
                gsend(h, 0, 0, lead[s] if turn == 0 else 1 - lead[s], 1, s)
    for c in loads[1:]:
        c.start()
    wocopy = pltpu.make_async_copy(woh, wo, misc.at[2])
    wocopy.start()

    def place(dim, shape):
        i = lax.broadcasted_iota(jnp.int32, shape, dim)
        blk = i // ROWS
        dx, dy = blk & 3, blk // RING
        return (
            ((((x + dx) & 3) * RING + ((y + dy) & 3)) * ROWS + (i & (ROWS - 1)))
        ).astype(F32)

    diff = place(0, (BLOCK, BLOCK)) - place(1, (BLOCK, BLOCK))
    pos = place(0, (BLOCK, HD))
    for h in range(2):
        r = rate[h]
        mask[h] = jnp.where(diff >= 0.0, jnp.exp(-r * jnp.maximum(diff, 0.0)), 0.0)
        odec[h] = jnp.exp(-r * (BLOCK - 1.0 - pos))
        idec[h] = jnp.exp(-r * (pos + 1.0))
    acc[...] = jnp.zeros_like(acc)

    def reorder(c):
        loads[c].wait()
        each = wrows // 512

        def body(i, carry):
            for u in range(2):
                n = c * each + i * 2 + u
                v = w2[pl.ds(pl.multiple_of(n * 512, 512), 512), :].astype(F32)
                v = jnp.transpose(v.reshape(64, 8, 128), (1, 0, 2))
                r0 = pl.multiple_of(n * 64, 64)
                for e in range(8):
                    col = SLOT[e % 4] * 256 + (e // 4) * 128
                    wf[pl.ds(r0, 64), pl.ds(col, 128)] = v[e].astype(BF)
            return carry

        lax.fori_loop(0, each // 2, body, 0)

    def project(h, g, n):
        cols = pl.ds(n * 512, 512)
        got = jnp.dot(
            xg[h][pl.ds(g * 128, 128), :], wf[pl.ds(h * half, half), cols],
            preferred_element_type=F32,
        )
        if h == 0:
            acc[pl.ds(g * 128, 128), cols] += got
        else:
            for e in range(2):
                for dp in range(RING):
                    at = (e * RING + dp) * ROWS
                    acc[pl.ds((dp * RING + g * 2 + e) * ROWS, ROWS), cols] += got[at:at + ROWS]

    reorder(0)
    reorder(1)
    for h in range(2):
        for dp, q, s in ((3, 0, 1), (1, 1, -1)):
            gwait(h, dp, 0, q)
            gsend(h, dp, 0, q, 0, s)
            gsend(h, dp, 0, q, 1, 1)
            gsend(h, dp, 0, q, 1, -1)
    reorder(2)
    for h in range(2):
        for dq, q, s in ((3, 0, 1), (1, 1, -1)):
            gwait(h, 0, dq, q)
            gsend(h, 0, dq, q, 1, s)
        for dp, q in ((3, 1), (1, 0)):
            gwait(h, dp, 0, q)
            gsend(h, dp, 0, q, 1, 1)
            gsend(h, dp, 0, q, 1, -1)
    reorder(3)
    for h in range(2):
        for q in range(2):
            gwait(h, 2, 0, q)
            gsend(h, 2, 0, q, 1, 1)
            gsend(h, 2, 0, q, 1, -1)
    reorder(4)
    for dp in (3, 1):
        for h in range(2):
            for dq, q, s in ((3, 0, 1), (1, 1, -1)):
                gwait(h, dp, dq, q)
                gsend(h, dp, dq, q, 1, s)
    reorder(5)
    for h in range(2):
        for dq, q, s in ((3, 0, 1), (1, 1, -1)):
            gwait(h, 2, dq, q)
            gsend(h, 2, dq, q, 1, s)
    for c in owns:
        c.wait()
    for h in range(2):
        for dp in (0, 3, 1, 2):
            gwait(h, dp, 1, 0)
        for n in range(2):
            project(h, 0, n)
    for h in range(2):
        for dp in (0, 3, 1, 2):
            gwait(h, dp, 3, 1)
        for dp in (0, 3, 1, 2):
            for q in range(2):
                gwait(h, dp, 2, q)
        project(h, 1, 0)

    def silu(v):
        return v / (1.0 + jnp.exp(-v))

    kb[...] = silu(acc[:, 0:256]).astype(BF)
    vb[...] = silu(acc[:, 256:512]).astype(BF)
    for h in range(2):
        cols = pl.ds(h * HD, HD)
        ks = (kb[:, cols].astype(F32) * odec[h]).astype(BF)
        st = lax.dot_general(
            ks, vb[:, cols], (((0,), (0,)), ((), ())), preferred_element_type=F32
        )
        sloc[h] = st
        sbf[h] = st.astype(BF)

    def pair(src, dst, n, where):
        return pltpu.make_async_remote_copy(
            src_ref=src, dst_ref=dst, send_sem=sts.at[n], recv_sem=str_.at[n],
            device_id={"seq": where}, device_id_type=MESH,
        )

    swap = pair(sbf, spart, 0, partner)
    swap.start()
    project(0, 1, 1)

    def inner(h):
        cols = pl.ds(h * HD, HD)
        sc = lax.dot_general(
            qb[:, cols], kb[:, cols], (((1,), (1,)), ((), ())), preferred_element_type=F32
        )
        wt = (sc * mask[h]).astype(BF)
        ab[:, cols] = jnp.dot(wt, vb[:, cols], preferred_element_type=F32)

    def decay(r, n):
        return jnp.exp(jnp.full((1, HD), -r * n, F32))

    swap.wait()
    mine, other = sloc[core], spart[core].astype(F32)
    fall = decay(rate[core], float(BLOCK))
    first = core == 0
    one = jnp.ones_like(fall)
    chip = jnp.where(first, fall, one) * mine + jnp.where(first, one, fall) * other
    tsend[...] = chip.astype(BF)
    for dz in (1, 2, 3):
        @pl.when(z + dz < RING)
        def _(dz=dz):
            pair(tsend, tbuf.at[dz - 1], dz, zpeer(dz)).start()

    project(1, 1, 1)
    qb[...] = silu(acc[:, 512:768]).astype(BF)
    inner(0)
    inner(1)
    gate = 1.0 / (1.0 + jnp.exp(-acc[:, 768:1024]))
    acc[:, 768:1024] = gate * gain[...]
    inc[...] = jnp.zeros_like(inc)
    for dz in (1, 2, 3):
        @pl.when(z >= dz)
        def _(dz=dz):
            pair(tsend, tbuf.at[dz - 1], dz, zpeer(dz)).wait_recv()
            inc[...] += decay(rate[core], float(2 * BLOCK * (dz - 1))) * tbuf[dz - 1].astype(F32)

    isend[...] = inc[...].astype(BF)
    back = pair(isend, ibuf, 4, partner)
    back.start()
    back.wait()
    wocopy.wait()
    own_in, far_in = isend[...].astype(F32), ibuf[...].astype(F32)
    for h in range(2):
        cols = pl.ds(h * HD, HD)
        chipin = jnp.where(core == h, own_in, far_in)
        fallh = decay(rate[h], float(BLOCK))
        state = jnp.where(first, chipin, fallh * chipin + spart[h].astype(F32))
        carried = jnp.dot(qb[:, cols], state.astype(BF), preferred_element_type=F32)
        attn = ab[:, cols] + carried * idec[h]
        square = jnp.mean(attn * attn, axis=-1, keepdims=True)
        ybuf[:, cols] = (
            attn * lax.rsqrt(square + 1e-06) * acc[:, pl.ds(768 + h * HD, HD)]
        ).astype(BF)

    def blk(h, dp, dq):
        return (dq * RING + dp if h == 0 else dp * RING + dq) * ROWS

    def outproj(h, dq):
        if h == 0:
            rows = ybuf[pl.ds(dq * 64, 64), :]
        else:
            rows = jnp.concatenate([ybuf[pl.ds(blk(1, dp, dq), ROWS), :] for dp in range(RING)], axis=0)
        got = jnp.dot(rows, wo[:, pl.ds(h * half, half)], preferred_element_type=F32).astype(BF)
        for dp in range(RING):
            part[h][pl.ds(blk(h, dp, dq), ROWS), :] = got[dp * ROWS:(dp + 1) * ROWS]

    def piece(h, dp, dq, q):
        return part[h].at[pl.ds(blk(h, dp, dq), ROWS), pl.ds(q * quart, quart)]

    def rsend(h, dp, dq, q, n, along, s):
        axis = (prim if along == 0 else sec)[h]
        push(
            piece(h, dp, dq, q), rb.at[h * 30 + n], rss.at[count[1]], rsr.at[h * 30 + n],
            {"tp": near[axis, s]},
        )
        count[1] += 1

    def rwait(h, n):
        pltpu.make_async_remote_copy(
            src_ref=rb.at[h * 30 + n], dst_ref=rb.at[h * 30 + n],
            send_sem=rss.at[0], recv_sem=rsr.at[h * 30 + n],
            device_id={"tp": near["x", 1]}, device_id_type=MESH,
        ).wait_recv()
        return rb[h * 30 + n].astype(F32)

    def n_opp(dp, side):
        return dp * 2 + side

    def n_in(dp, side, q):
        return 8 + dp * 4 + side * 2 + q

    def opposite(h, dp):
        rsend(h, dp, 2, 0, n_opp(dp, 0), 1, 1)
        rsend(h, dp, 2, 1, n_opp(dp, 1), 1, -1)

    def direct(h, dp):
        rsend(h, dp, 1, 1, n_in(dp, 0, 1), 1, 1)
        rsend(h, dp, 3, 0, n_in(dp, 1, 0), 1, -1)

    def merged(h, dp):
        for dq, q, side, s in ((1, 0, 0, 1), (3, 1, 1, -1)):
            got = rwait(h, n_opp(dp, side))
            p = piece(h, dp, dq, q)
            p[...] = (p[...].astype(F32) + got).astype(BF)
            rsend(h, dp, dq, q, n_in(dp, side, q), 1, s)

    def gathered(h, dp, q):
        return (
            piece(h, dp, 0, q)[...].astype(F32)
            + rwait(h, n_in(dp, 0, q)) + rwait(h, n_in(dp, 1, q))
        )

    for h in range(2):
        outproj(h, 2)
    for h in range(2):
        opposite(h, 2)
    for h in range(2):
        outproj(h, 1)
        outproj(h, 3)
    for h in range(2):
        direct(h, 2)
        opposite(h, 1)
        opposite(h, 3)
    for h in range(2):
        outproj(h, 0)
    for h in range(2):
        merged(h, 2)
    for h in range(2):
        direct(h, 1)
        direct(h, 3)
        opposite(h, 0)
    for dp in (1, 3):
        for h in range(2):
            merged(h, dp)
    for h in range(2):
        for q, s in ((0, 1), (1, -1)):
            piece(h, 2, 0, q)[...] = gathered(h, 2, q).astype(BF)
            rsend(h, 2, 0, q, 24 + q, 0, s)
    for h in range(2):
        direct(h, 0)
    for h in range(2):
        merged(h, 0)
    for h in range(2):
        for dp, q, side, s in ((1, 1, 0, 1), (3, 0, 1, -1)):
            piece(h, dp, 0, q)[...] = gathered(h, dp, q).astype(BF)
            rsend(h, dp, 0, q, 26 + side * 2 + q, 0, s)
    for h in range(2):
        for dp, q, side, s in ((1, 0, 0, 1), (3, 1, 1, -1)):
            got = gathered(h, dp, q) + rwait(h, 24 + side)
            piece(h, dp, 0, q)[...] = got.astype(BF)
            rsend(h, dp, 0, q, 26 + side * 2 + q, 0, s)
    for h in range(2):
        for q in range(2):
            got = gathered(h, 0, q) + rwait(h, 26 + q) + rwait(h, 28 + q)
            out[:, pl.ds(h * half + q * quart, quart)] = got.astype(BF)

    for c in sent:
        c.wait_send()
    for dz in (1, 2, 3):
        @pl.when(z + dz < RING)
        def _(dz=dz):
            pair(tsend, tbuf.at[dz - 1], dz, zpeer(dz)).wait_send()


def per_device(tokens, proj_weight, out_weight, head_gain, decay_rate):
    d = tokens.shape[1]
    w2 = proj_weight.reshape(d, 4, 2, HD).transpose(0, 2, 1, 3).reshape(d * 8, HD)
    anyspace = pl.BlockSpec(memory_space=pl.ANY)
    vmem = pl.BlockSpec(memory_space=pltpu.VMEM)
    dma = pltpu.SemaphoreType.DMA
    v = pltpu.VMEM
    half = d // 2
    scratch = [
        v((BLOCK, half), BF), v((BLOCK, half), BF),
        v((d * 8, HD), BF), v((d, 1024), BF), v((256, d), BF),
        v((BLOCK, 1024), F32),
        v((2, BLOCK, BLOCK), F32), v((2, BLOCK, HD), F32), v((2, BLOCK, HD), F32),
        v((BLOCK, 256), BF), v((BLOCK, 256), BF), v((BLOCK, 256), BF),
        v((BLOCK, 256), F32), v((BLOCK, 256), BF),
        v((BLOCK, half), BF), v((BLOCK, half), BF),
        v((60, ROWS, half // 2), BF),
        v((2, HD, HD), F32), v((2, HD, HD), BF), v((2, HD, HD), BF),
        v((HD, HD), BF), v((3, HD, HD), BF), v((HD, HD), F32),
        v((HD, HD), BF), v((HD, HD), BF),
        dma((60,)), dma((60,)), dma((60,)), dma((60,)),
        dma((WCHUNKS,)), dma((3,)), dma((5,)), dma((5,)),
    ]
    return pl.pallas_call(
        fused,
        name="fused_layer",
        out_shape=jax.ShapeDtypeStruct(tokens.shape, BF),
        in_specs=[anyspace, anyspace, anyspace, vmem, pl.BlockSpec(memory_space=pltpu.SMEM)],
        out_specs=vmem,
        scratch_shapes=scratch,
        compiler_params=pltpu.CompilerParams(
            collective_id=0, has_side_effects=True, vmem_limit_bytes=60 * 1024 * 1024
        ),
    )(tokens, w2, out_weight, head_gain.reshape(1, -1), decay_rate)


def solution(mesh):
    return jax.shard_map(
        per_device,
        mesh=mesh,
        in_specs=(P(("seq", "tp"), None), P(None, None, "tp"), P("tp", None), P("tp"), P("tp")),
        out_specs=P(("seq", "tp"), None),
        check_vma=False,
    )
```

```python
import jax
import jax.numpy as jnp
from jax import lax
from jax.experimental import pallas as pl
from jax.experimental.pallas import tpu as pltpu
from jax.sharding import PartitionSpec as P

HD = 128
ROWS = 16
BLOCK = 256
RING = 4
WCHUNKS = 6
SLOT = (2, 0, 1, 3)
BF = jnp.bfloat16
F32 = jnp.float32
MESH = pl.DeviceIdType.MESH


def fused(
    tok, w2h, woh, gainh, rateh, outh,
    xga, xgb, w2, wf, wo, acc, mask, odec, idec, qb, kb, vb, ab, ybuf, pa, pb, rb,
    sloc, sbf, spart, tsend, tbuf, inc, isend, ibuf,
    out, gain, rate, ags, agr, rss, rsr, ws, misc, sts, str_,
):
    d = tok.shape[1]
    half = d // 2
    quart = half // 2
    seq = lax.axis_index("seq")
    tp = lax.axis_index("tp")
    z, core = seq // 2, lax.rem(seq, 2)
    x, y = tp // RING, lax.rem(tp, RING)

    def shift(v, s):
        return lax.rem(v + (s + RING), RING)

    near = {
        ("x", s): shift(x, s) * RING + y for s in (1, -1)
    } | {("y", s): x * RING + shift(y, s) for s in (1, -1)}
    prim, sec = ("x", "y"), ("y", "x")
    xg, part = (xga, xgb), (pa, pb)
    partner = z * 2 + (1 - core)

    def zpeer(dz):
        return lax.rem(z + dz, RING) * 2 + core

    barrier = pltpu.get_barrier_semaphore()
    for where in near.values():
        pl.semaphore_signal(barrier, inc=1, device_id={"tp": where}, device_id_type=MESH)
    for where in (partner, zpeer(1), zpeer(2), zpeer(3)):
        pl.semaphore_signal(barrier, inc=1, device_id={"seq": where}, device_id_type=MESH)

    small = [
        pltpu.make_async_copy(rateh, rate, misc.at[3]),
        pltpu.make_async_copy(gainh, gain, misc.at[4]),
    ]
    for c in small:
        c.start()
    wrows = w2.shape[0] // WCHUNKS
    loads = [
        pltpu.make_async_copy(
            w2h.at[pl.ds(c * wrows, wrows)], w2.at[pl.ds(c * wrows, wrows)], ws.at[c]
        )
        for c in range(WCHUNKS)
    ]
    loads[0].start()
    owns = [
        pltpu.make_async_copy(
            tok.at[:, pl.ds(h * half, half)], xg[h].at[pl.ds(0, ROWS)], misc.at[h]
        )
        for h in range(2)
    ]
    for c in owns:
        c.start()
    pl.semaphore_wait(barrier, 8)

    sent = []

    def push(src, dst, ssem, rsem, where):
        c = pltpu.make_async_remote_copy(
            src_ref=src, dst_ref=dst, send_sem=ssem, recv_sem=rsem,
            device_id=where, device_id_type=MESH,
        )
        c.start()
        sent.append(c)

    def spot(h, dp, dq, q):
        return xg[h].at[pl.ds((dq * RING + dp) * ROWS, ROWS), pl.ds(q * quart, quart)]

    def key(h, dp, dq, q):
        return h * 30 + (dq * RING + dp - 1) * 2 + q

    count = [0, 0]

    def gsend(h, dp, dq, q, along, s):
        if dp == 0 and dq == 0:
            src = tok.at[:, pl.ds(h * half + q * quart, quart)]
        else:
            src = spot(h, dp, dq, q)
        if along == 0:
            ndp, ndq, axis = (dp - s) % RING, dq, prim[h]
        else:
            ndp, ndq, axis = dp, (dq - s) % RING, sec[h]
        push(
            src, spot(h, ndp, ndq, q), ags.at[count[0]], agr.at[key(h, ndp, ndq, q)],
            {"tp": near[axis, s]},
        )
        count[0] += 1

    def gwait(h, dp, dq, q):
        pltpu.make_async_remote_copy(
            src_ref=spot(h, dp, dq, q), dst_ref=spot(h, dp, dq, q),
            send_sem=ags.at[0], recv_sem=agr.at[key(h, dp, dq, q)],
            device_id={"tp": near["x", 1]}, device_id_type=MESH,
        ).wait_recv()

    lead = {1: 0, -1: 1}
    for turn in range(2):
        for h in range(2):
            for s in (1, -1):
                gsend(h, 0, 0, lead[s] if turn == 0 else 1 - lead[s], 0, s)
    for turn in range(2):
        for h in range(2):
            for s in (1, -1):
                gsend(h, 0, 0, lead[s] if turn == 0 else 1 - lead[s], 1, s)
    for c in loads[1:]:
        c.start()
    wocopy = pltpu.make_async_copy(woh, wo, misc.at[2])
    wocopy.start()
    for c in small:
        c.wait()

    def place(dim, shape):
        i = lax.broadcasted_iota(jnp.int32, shape, dim)
        blk = i // ROWS
        dx, dy = blk & 3, blk // RING
        return (
            ((((x + dx) & 3) * RING + ((y + dy) & 3)) * ROWS + (i & (ROWS - 1)))
        ).astype(F32)

    diff = place(0, (BLOCK, BLOCK)) - place(1, (BLOCK, BLOCK))
    pos = place(0, (BLOCK, HD))
    for h in range(2):
        r = rate[h]
        mask[h] = jnp.where(diff >= 0.0, jnp.exp(-r * jnp.maximum(diff, 0.0)), 0.0)
        odec[h] = jnp.exp(-r * (BLOCK - 1.0 - pos))
        idec[h] = jnp.exp(-r * (pos + 1.0))
    acc[...] = jnp.zeros_like(acc)

    def reorder(c):
        loads[c].wait()
        each = wrows // 512

        def body(i, carry):
            for u in range(2):
                n = c * each + i * 2 + u
                v = w2[pl.ds(pl.multiple_of(n * 512, 512), 512), :].astype(F32)
                v = jnp.transpose(v.reshape(64, 8, 128), (1, 0, 2))
                r0 = pl.multiple_of(n * 64, 64)
                for e in range(8):
                    col = SLOT[e % 4] * 256 + (e // 4) * 128
                    wf[pl.ds(r0, 64), pl.ds(col, 128)] = v[e].astype(BF)
            return carry

        lax.fori_loop(0, each // 2, body, 0)

    def project(h, g, n):
        cols = pl.ds(n * 512, 512)
        got = jnp.dot(
            xg[h][pl.ds(g * 128, 128), :], wf[pl.ds(h * half, half), cols],
            preferred_element_type=F32,
        )
        if h == 0:
            acc[pl.ds(g * 128, 128), cols] += got
        else:
            for e in range(2):
                for dp in range(RING):
                    at = (e * RING + dp) * ROWS
                    acc[pl.ds((dp * RING + g * 2 + e) * ROWS, ROWS), cols] += got[at:at + ROWS]

    reorder(0)
    reorder(1)
    for h in range(2):
        for dp, q, s in ((3, 0, 1), (1, 1, -1)):
            gwait(h, dp, 0, q)
            gsend(h, dp, 0, q, 0, s)
            gsend(h, dp, 0, q, 1, 1)
            gsend(h, dp, 0, q, 1, -1)
    reorder(2)
    for h in range(2):
        for dq, q, s in ((3, 0, 1), (1, 1, -1)):
            gwait(h, 0, dq, q)
            gsend(h, 0, dq, q, 1, s)
        for dp, q in ((3, 1), (1, 0)):
            gwait(h, dp, 0, q)
            gsend(h, dp, 0, q, 1, 1)
            gsend(h, dp, 0, q, 1, -1)
    reorder(3)
    for h in range(2):
        for q in range(2):
            gwait(h, 2, 0, q)
            gsend(h, 2, 0, q, 1, 1)
            gsend(h, 2, 0, q, 1, -1)
    reorder(4)
    for dp in (3, 1):
        for h in range(2):
            for dq, q, s in ((3, 0, 1), (1, 1, -1)):
                gwait(h, dp, dq, q)
                gsend(h, dp, dq, q, 1, s)
    reorder(5)
    for h in range(2):
        for dq, q, s in ((3, 0, 1), (1, 1, -1)):
            gwait(h, 2, dq, q)
            gsend(h, 2, dq, q, 1, s)
    for c in owns:
        c.wait()
    for h in range(2):
        for dp in (0, 3, 1, 2):
            gwait(h, dp, 1, 0)
        for n in range(2):
            project(h, 0, n)
    for h in range(2):
        for dp in (0, 3, 1, 2):
            gwait(h, dp, 3, 1)
        for dp in (0, 3, 1, 2):
            for q in range(2):
                gwait(h, dp, 2, q)
        project(h, 1, 0)

    def silu(v):
        return v / (1.0 + jnp.exp(-v))

    kb[...] = silu(acc[:, 0:256]).astype(BF)
    vb[...] = silu(acc[:, 256:512]).astype(BF)
    for h in range(2):
        cols = pl.ds(h * HD, HD)
        ks = (kb[:, cols].astype(F32) * odec[h]).astype(BF)
        st = lax.dot_general(
            ks, vb[:, cols], (((0,), (0,)), ((), ())), preferred_element_type=F32
        )
        sloc[h] = st
        sbf[h] = st.astype(BF)

    def pair(src, dst, n, where):
        return pltpu.make_async_remote_copy(
            src_ref=src, dst_ref=dst, send_sem=sts.at[n], recv_sem=str_.at[n],
            device_id={"seq": where}, device_id_type=MESH,
        )

    swap = pair(sbf.at[1 - core], spart.at[1 - core], 0, partner)
    rest = pair(sbf.at[core], spart.at[core], 5, partner)
    swap.start()
    rest.start()
    project(0, 1, 1)

    def inner(h):
        cols = pl.ds(h * HD, HD)
        sc = lax.dot_general(
            qb[:, cols], kb[:, cols], (((1,), (1,)), ((), ())), preferred_element_type=F32
        )
        wt = (sc * mask[h]).astype(BF)
        ab[:, cols] = jnp.dot(wt, vb[:, cols], preferred_element_type=F32)

    def decay(r, n):
        return jnp.exp(jnp.full((1, HD), -r * n, F32))

    pltpu.make_async_remote_copy(
        src_ref=sbf.at[1 - core], dst_ref=spart.at[core], send_sem=sts.at[0], recv_sem=str_.at[0],
        device_id={"seq": partner}, device_id_type=MESH,
    ).wait()
    mine, other = sloc[core], spart[core].astype(F32)
    fall = decay(rate[core], float(BLOCK))
    first = core == 0
    one = jnp.ones_like(fall)
    chip = jnp.where(first, fall, one) * mine + jnp.where(first, one, fall) * other
    tsend[...] = chip.astype(BF)
    for dz in (1, 2, 3):
        @pl.when(z + dz < RING)
        def _(dz=dz):
            pair(tsend, tbuf.at[dz - 1], dz, zpeer(dz)).start()

    project(1, 1, 1)
    qb[...] = silu(acc[:, 512:768]).astype(BF)
    inner(0)
    inner(1)
    gate = 1.0 / (1.0 + jnp.exp(-acc[:, 768:1024]))
    acc[:, 768:1024] = gate * gain[...]
    inc[...] = jnp.zeros_like(inc)
    for dz in (1, 2, 3):
        @pl.when(z >= dz)
        def _(dz=dz):
            pair(tsend, tbuf.at[dz - 1], dz, zpeer(dz)).wait_recv()
            inc[...] += decay(rate[core], float(2 * BLOCK * (dz - 1))) * tbuf[dz - 1].astype(F32)

    isend[...] = inc[...].astype(BF)
    back = pair(isend, ibuf, 4, partner)
    back.start()
    wocopy.wait()

    def finish(h, into):
        cols = pl.ds(pl.multiple_of(h * HD, HD), HD)
        chipin = into[...].astype(F32)
        fallh = decay(rate[h], float(BLOCK))
        state = jnp.where(first, chipin, fallh * chipin + spart[h].astype(F32))
        carried = jnp.dot(qb[:, cols], state.astype(BF), preferred_element_type=F32)
        attn = ab[:, cols] + carried * idec[h]
        square = jnp.mean(attn * attn, axis=-1, keepdims=True)
        gated = acc[:, pl.ds(pl.multiple_of(768 + h * HD, HD), HD)]
        ybuf[:, cols] = (attn * lax.rsqrt(square + 1e-06) * gated).astype(BF)

    pltpu.make_async_remote_copy(
        src_ref=sbf.at[core], dst_ref=spart.at[1 - core], send_sem=sts.at[5], recv_sem=str_.at[5],
        device_id={"seq": partner}, device_id_type=MESH,
    ).wait()
    finish(core, isend)
    back.wait()
    finish(1 - core, ibuf)

    def blk(h, dp, dq):
        return (dq * RING + dp if h == 0 else dp * RING + dq) * ROWS

    def outproj(h, dq):
        if h == 0:
            rows = ybuf[pl.ds(dq * 64, 64), :]
        else:
            rows = jnp.concatenate([ybuf[pl.ds(blk(1, dp, dq), ROWS), :] for dp in range(RING)], axis=0)
        got = jnp.dot(rows, wo[:, pl.ds(h * half, half)], preferred_element_type=F32).astype(BF)
        for dp in range(RING):
            part[h][pl.ds(blk(h, dp, dq), ROWS), :] = got[dp * ROWS:(dp + 1) * ROWS]

    def piece(h, dp, dq, q):
        return part[h].at[pl.ds(blk(h, dp, dq), ROWS), pl.ds(q * quart, quart)]

    def rsend(h, dp, dq, q, n, along, s):
        axis = (prim if along == 0 else sec)[h]
        push(
            piece(h, dp, dq, q), rb.at[h * 30 + n], rss.at[count[1]], rsr.at[h * 30 + n],
            {"tp": near[axis, s]},
        )
        count[1] += 1

    def rwait(h, n):
        pltpu.make_async_remote_copy(
            src_ref=rb.at[h * 30 + n], dst_ref=rb.at[h * 30 + n],
            send_sem=rss.at[0], recv_sem=rsr.at[h * 30 + n],
            device_id={"tp": near["x", 1]}, device_id_type=MESH,
        ).wait_recv()
        return rb[h * 30 + n].astype(F32)

    def n_opp(dp, side):
        return dp * 2 + side

    def n_in(dp, side, q):
        return 8 + dp * 4 + side * 2 + q

    def opposite(h, dp):
        rsend(h, dp, 2, 0, n_opp(dp, 0), 1, 1)
        rsend(h, dp, 2, 1, n_opp(dp, 1), 1, -1)

    def direct(h, dp):
        rsend(h, dp, 1, 1, n_in(dp, 0, 1), 1, 1)
        rsend(h, dp, 3, 0, n_in(dp, 1, 0), 1, -1)

    def merged(h, dp):
        for dq, q, side, s in ((1, 0, 0, 1), (3, 1, 1, -1)):
            got = rwait(h, n_opp(dp, side))
            p = piece(h, dp, dq, q)
            p[...] = (p[...].astype(F32) + got).astype(BF)
            rsend(h, dp, dq, q, n_in(dp, side, q), 1, s)

    def gathered(h, dp, q):
        return (
            piece(h, dp, 0, q)[...].astype(F32)
            + rwait(h, n_in(dp, 0, q)) + rwait(h, n_in(dp, 1, q))
        )

    for h in range(2):
        outproj(h, 2)
        opposite(h, 2)
    for h in range(2):
        opposite(h, 1)
    for h in range(2):
        outproj(h, 1)
        outproj(h, 3)
        direct(h, 2)
    for h in range(2):
        opposite(h, 3)
    for h in range(2):
        outproj(h, 0)
    for h in range(2):
        merged(h, 2)
    for h in range(2):
        direct(h, 1)
        direct(h, 3)
        opposite(h, 0)
    for dp in (1, 3):
        for h in range(2):
            merged(h, dp)
    for h in range(2):
        for q, s in ((0, 1), (1, -1)):
            piece(h, 2, 0, q)[...] = gathered(h, 2, q).astype(BF)
            rsend(h, 2, 0, q, 24 + q, 0, s)
    for h in range(2):
        direct(h, 0)
    for h in range(2):
        merged(h, 0)
    for h in range(2):
        for dp, q, side, s in ((1, 1, 0, 1), (3, 0, 1, -1)):
            piece(h, dp, 0, q)[...] = gathered(h, dp, q).astype(BF)
            rsend(h, dp, 0, q, 26 + side * 2 + q, 0, s)
    for h in range(2):
        for dp, q, side, s in ((1, 0, 0, 1), (3, 1, 1, -1)):
            got = gathered(h, dp, q) + rwait(h, 24 + side)
            piece(h, dp, 0, q)[...] = got.astype(BF)
            rsend(h, dp, 0, q, 26 + side * 2 + q, 0, s)
    puts = []
    for h in range(2):
        for q in range(2):
            got = gathered(h, 0, q) + rwait(h, 26 + q) + rwait(h, 28 + q)
            cols = pl.ds(h * half + q * quart, quart)
            out[:, cols] = got.astype(BF)
            puts.append(pltpu.make_async_copy(out.at[:, cols], outh.at[:, cols], misc.at[5 + h * 2 + q]))
            puts[-1].start()

    for c in sent:
        c.wait_send()
    for c in puts:
        c.wait()
    for dz in (1, 2, 3):
        @pl.when(z + dz < RING)
        def _(dz=dz):
            pair(tsend, tbuf.at[dz - 1], dz, zpeer(dz)).wait_send()


def per_device(tokens, proj_weight, out_weight, head_gain, decay_rate):
    d = tokens.shape[1]
    w2 = proj_weight.reshape(d, 4, 2, HD).transpose(0, 2, 1, 3).reshape(d * 8, HD)
    anyspace = pl.BlockSpec(memory_space=pl.ANY)
    far = pl.BlockSpec(memory_space=pltpu.HBM)
    vmem = pl.BlockSpec(memory_space=pltpu.VMEM)
    dma = pltpu.SemaphoreType.DMA
    v = pltpu.VMEM
    half = d // 2
    scratch = [
        v((BLOCK, half), BF), v((BLOCK, half), BF),
        v((d * 8, HD), BF), v((d, 1024), BF), v((256, d), BF),
        v((BLOCK, 1024), F32),
        v((2, BLOCK, BLOCK), F32), v((2, BLOCK, HD), F32), v((2, BLOCK, HD), F32),
        v((BLOCK, 256), BF), v((BLOCK, 256), BF), v((BLOCK, 256), BF),
        v((BLOCK, 256), F32), v((BLOCK, 256), BF),
        v((BLOCK, half), BF), v((BLOCK, half), BF),
        v((60, ROWS, half // 2), BF),
        v((2, HD, HD), F32), v((2, HD, HD), BF), v((2, HD, HD), BF),
        v((HD, HD), BF), v((3, HD, HD), BF), v((HD, HD), F32),
        v((HD, HD), BF), v((HD, HD), BF),
        v((ROWS, d), BF), v((1, 2 * HD), F32), pltpu.SMEM((2,), F32),
        dma((60,)), dma((60,)), dma((60,)), dma((60,)),
        dma((WCHUNKS,)), dma((9,)), dma((6,)), dma((6,)),
    ]
    return pl.pallas_call(
        fused,
        name="fused_layer",
        out_shape=jax.ShapeDtypeStruct(tokens.shape, BF),
        in_specs=[far] * 5,
        out_specs=anyspace,
        scratch_shapes=scratch,
        compiler_params=pltpu.CompilerParams(
            collective_id=0, has_side_effects=True, vmem_limit_bytes=52 * 1024 * 1024
        ),
    )(*(
        pltpu.with_memory_space_constraint(a, pltpu.HBM)
        for a in (tokens, w2, out_weight, head_gain.reshape(1, -1), decay_rate)
    ))


def solution(mesh):
    return jax.shard_map(
        per_device,
        mesh=mesh,
        in_specs=(P(("seq", "tp"), None), P(None, None, "tp"), P("tp", None), P("tp"), P("tp")),
        out_specs=P(("seq", "tp"), None),
        check_vma=False,
    )
```

```python
import jax
import jax.numpy as jnp
from jax import lax
from jax.experimental import pallas as pl
from jax.experimental.pallas import tpu as pltpu
from jax.sharding import PartitionSpec as P

HD = 128
ROWS = 16
BLOCK = 256
RING = 4
WCHUNKS = 6
SLOT = (2, 0, 1, 3)
BF = jnp.bfloat16
F32 = jnp.float32
MESH = pl.DeviceIdType.MESH


def fused(
    tok, w2h, woh, gainh, rateh, outh,
    xga, xgb, w2, wf, wo, acc, mask, odec, idec, qb, kb, vb, ab, ybuf, pa, pb, rb,
    sloc, sbf, spart, tsend, tbuf, inc, isend, ibuf,
    out, gain, rate, ags, agr, rss, rsr, ws, misc, sts, str_,
):
    d = tok.shape[1]
    half = d // 2
    quart = half // 2
    seq = lax.axis_index("seq")
    tp = lax.axis_index("tp")
    z, core = seq // 2, lax.rem(seq, 2)
    x, y = tp // RING, lax.rem(tp, RING)

    def shift(v, s):
        return lax.rem(v + (s + RING), RING)

    near = {
        ("x", s): shift(x, s) * RING + y for s in (1, -1)
    } | {("y", s): x * RING + shift(y, s) for s in (1, -1)}
    prim, sec = ("x", "y"), ("y", "x")
    xg, part = (xga, xgb), (pa, pb)
    partner = z * 2 + (1 - core)

    def zpeer(dz):
        return lax.rem(z + dz, RING) * 2 + core

    barrier = pltpu.get_barrier_semaphore()
    for where in near.values():
        pl.semaphore_signal(barrier, inc=1, device_id={"tp": where}, device_id_type=MESH)
    for where in (partner, zpeer(1), zpeer(2), zpeer(3)):
        pl.semaphore_signal(barrier, inc=1, device_id={"seq": where}, device_id_type=MESH)

    small = [
        pltpu.make_async_copy(rateh, rate, misc.at[3]),
        pltpu.make_async_copy(gainh, gain, misc.at[4]),
    ]
    for c in small:
        c.start()
    wrows = w2.shape[0] // WCHUNKS
    loads = [
        pltpu.make_async_copy(
            w2h.at[pl.ds(c * wrows, wrows)], w2.at[pl.ds(c * wrows, wrows)], ws.at[c]
        )
        for c in range(WCHUNKS)
    ]
    loads[0].start()
    owns = [
        pltpu.make_async_copy(
            tok.at[:, pl.ds(h * half, half)], xg[h].at[pl.ds(0, ROWS)], misc.at[h]
        )
        for h in range(2)
    ]
    for c in owns:
        c.start()
    pl.semaphore_wait(barrier, 8)

    sent = []

    def push(src, dst, ssem, rsem, where):
        c = pltpu.make_async_remote_copy(
            src_ref=src, dst_ref=dst, send_sem=ssem, recv_sem=rsem,
            device_id=where, device_id_type=MESH,
        )
        c.start()
        sent.append(c)

    def spot(h, dp, dq, q):
        return xg[h].at[pl.ds((dq * RING + dp) * ROWS, ROWS), pl.ds(q * quart, quart)]

    def key(h, dp, dq, q):
        return h * 30 + (dq * RING + dp - 1) * 2 + q

    count = [0, 0]

    def gsend(h, dp, dq, q, along, s):
        if dp == 0 and dq == 0:
            src = tok.at[:, pl.ds(h * half + q * quart, quart)]
        else:
            src = spot(h, dp, dq, q)
        if along == 0:
            ndp, ndq, axis = (dp - s) % RING, dq, prim[h]
        else:
            ndp, ndq, axis = dp, (dq - s) % RING, sec[h]
        push(
            src, spot(h, ndp, ndq, q), ags.at[count[0]], agr.at[key(h, ndp, ndq, q)],
            {"tp": near[axis, s]},
        )
        count[0] += 1

    def gwait(h, dp, dq, q):
        pltpu.make_async_remote_copy(
            src_ref=spot(h, dp, dq, q), dst_ref=spot(h, dp, dq, q),
            send_sem=ags.at[0], recv_sem=agr.at[key(h, dp, dq, q)],
            device_id={"tp": near["x", 1]}, device_id_type=MESH,
        ).wait_recv()

    lead = {1: 0, -1: 1}
    for turn in range(2):
        for h in range(2):
            for s in (1, -1):
                gsend(h, 0, 0, lead[s] if turn == 0 else 1 - lead[s], 0, s)
    for turn in range(2):
        for h in range(2):
            for s in (1, -1):
                gsend(h, 0, 0, lead[s] if turn == 0 else 1 - lead[s], 1, s)
    for c in loads[1:]:
        c.start()
    wocopy = pltpu.make_async_copy(woh, wo, misc.at[2])
    wocopy.start()
    for c in small:
        c.wait()

    def place(dim, shape):
        i = lax.broadcasted_iota(jnp.int32, shape, dim)
        blk = i // ROWS
        dx, dy = blk & 3, blk // RING
        return (
            ((((x + dx) & 3) * RING + ((y + dy) & 3)) * ROWS + (i & (ROWS - 1)))
        ).astype(F32)

    diff = place(0, (BLOCK, BLOCK)) - place(1, (BLOCK, BLOCK))
    pos = place(0, (BLOCK, HD))
    for h in range(2):
        r = rate[h]
        mask[h] = jnp.where(diff >= 0.0, jnp.exp(-r * jnp.maximum(diff, 0.0)), 0.0)
        odec[h] = jnp.exp(-r * (BLOCK - 1.0 - pos))
        idec[h] = jnp.exp(-r * (pos + 1.0))
    acc[...] = jnp.zeros_like(acc)

    def reorder(c):
        loads[c].wait()
        each = wrows // 512

        def body(i, carry):
            for u in range(2):
                n = c * each + i * 2 + u
                v = w2[pl.ds(pl.multiple_of(n * 512, 512), 512), :].astype(F32)
                v = jnp.transpose(v.reshape(64, 8, 128), (1, 0, 2))
                r0 = pl.multiple_of(n * 64, 64)
                for e in range(8):
                    col = SLOT[e % 4] * 256 + (e // 4) * 128
                    wf[pl.ds(r0, 64), pl.ds(col, 128)] = v[e].astype(BF)
            return carry

        lax.fori_loop(0, each // 2, body, 0)

    def project(h, g, n):
        cols = pl.ds(n * 512, 512)
        got = jnp.dot(
            xg[h][pl.ds(g * 128, 128), :], wf[pl.ds(h * half, half), cols],
            preferred_element_type=F32,
        )
        if h == 0:
            acc[pl.ds(g * 128, 128), cols] += got
        else:
            for e in range(2):
                for dp in range(RING):
                    at = (e * RING + dp) * ROWS
                    acc[pl.ds((dp * RING + g * 2 + e) * ROWS, ROWS), cols] += got[at:at + ROWS]

    reorder(0)
    reorder(1)
    for h in range(2):
        for dp, q, s in ((3, 0, 1), (1, 1, -1)):
            gwait(h, dp, 0, q)
            gsend(h, dp, 0, q, 0, s)
            gsend(h, dp, 0, q, 1, 1)
            gsend(h, dp, 0, q, 1, -1)
    reorder(2)
    for h in range(2):
        for dq, q, s in ((3, 0, 1), (1, 1, -1)):
            gwait(h, 0, dq, q)
            gsend(h, 0, dq, q, 1, s)
        for dp, q in ((3, 1), (1, 0)):
            gwait(h, dp, 0, q)
            gsend(h, dp, 0, q, 1, 1)
            gsend(h, dp, 0, q, 1, -1)
    reorder(3)
    for h in range(2):
        for q in range(2):
            gwait(h, 2, 0, q)
            gsend(h, 2, 0, q, 1, 1)
            gsend(h, 2, 0, q, 1, -1)
    reorder(4)
    for dp in (3, 1):
        for h in range(2):
            for dq, q, s in ((3, 0, 1), (1, 1, -1)):
                gwait(h, dp, dq, q)
                gsend(h, dp, dq, q, 1, s)
    reorder(5)
    for h in range(2):
        for dq, q, s in ((3, 0, 1), (1, 1, -1)):
            gwait(h, 2, dq, q)
            gsend(h, 2, dq, q, 1, s)
    for c in owns:
        c.wait()
    for h in range(2):
        for dp in (0, 3, 1, 2):
            gwait(h, dp, 1, 0)
        for n in range(2):
            project(h, 0, n)
    for h in range(2):
        for dp in (0, 3, 1, 2):
            gwait(h, dp, 3, 1)
        for dp in (0, 3, 1, 2):
            for q in range(2):
                gwait(h, dp, 2, q)
        project(h, 1, 0)

    def silu(v):
        return v / (1.0 + jnp.exp(-v))

    kb[...] = silu(acc[:, 0:256]).astype(BF)
    vb[...] = silu(acc[:, 256:512]).astype(BF)
    for h in range(2):
        cols = pl.ds(h * HD, HD)
        ks = (kb[:, cols].astype(F32) * odec[h]).astype(BF)
        st = lax.dot_general(
            ks, vb[:, cols], (((0,), (0,)), ((), ())), preferred_element_type=F32
        )
        sloc[h] = st
        sbf[h] = st.astype(BF)

    def pair(src, dst, n, where):
        return pltpu.make_async_remote_copy(
            src_ref=src, dst_ref=dst, send_sem=sts.at[n], recv_sem=str_.at[n],
            device_id={"seq": where}, device_id_type=MESH,
        )

    swap = pair(sbf.at[1 - core], spart.at[1 - core], 0, partner)
    rest = pair(sbf.at[core], spart.at[core], 5, partner)
    swap.start()
    rest.start()
    project(0, 1, 1)

    def inner(h):
        cols = pl.ds(h * HD, HD)
        sc = lax.dot_general(
            qb[:, cols], kb[:, cols], (((1,), (1,)), ((), ())), preferred_element_type=F32
        )
        wt = (sc * mask[h]).astype(BF)
        ab[:, cols] = jnp.dot(wt, vb[:, cols], preferred_element_type=F32)

    def decay(r, n):
        return jnp.exp(jnp.full((1, HD), -r * n, F32))

    pltpu.make_async_remote_copy(
        src_ref=sbf.at[1 - core], dst_ref=spart.at[core], send_sem=sts.at[0], recv_sem=str_.at[0],
        device_id={"seq": partner}, device_id_type=MESH,
    ).wait()
    mine, other = sloc[core], spart[core].astype(F32)
    fall = decay(rate[core], float(BLOCK))
    first = core == 0
    one = jnp.ones_like(fall)
    chip = jnp.where(first, fall, one) * mine + jnp.where(first, one, fall) * other
    tsend[...] = chip.astype(BF)
    for dz in (1, 2, 3):
        @pl.when(z + dz < RING)
        def _(dz=dz):
            pair(tsend, tbuf.at[dz - 1], dz, zpeer(dz)).start()

    project(1, 1, 1)
    qb[...] = silu(acc[:, 512:768]).astype(BF)
    inner(0)
    inner(1)
    gate = 1.0 / (1.0 + jnp.exp(-acc[:, 768:1024]))
    acc[:, 768:1024] = gate * gain[...]
    inc[...] = jnp.zeros_like(inc)
    for dz in (1, 2, 3):
        @pl.when(z >= dz)
        def _(dz=dz):
            pair(tsend, tbuf.at[dz - 1], dz, zpeer(dz)).wait_recv()
            inc[...] += decay(rate[core], float(2 * BLOCK * (dz - 1))) * tbuf[dz - 1].astype(F32)

    isend[...] = inc[...].astype(BF)
    back = pair(isend, ibuf, 4, partner)
    back.start()
    wocopy.wait()

    def finish(h, into):
        cols = pl.ds(pl.multiple_of(h * HD, HD), HD)
        chipin = into[...].astype(F32)
        fallh = decay(rate[h], float(BLOCK))
        state = jnp.where(first, chipin, fallh * chipin + spart[h].astype(F32))
        carried = jnp.dot(qb[:, cols], state.astype(BF), preferred_element_type=F32)
        attn = ab[:, cols] + carried * idec[h]
        square = jnp.mean(attn * attn, axis=-1, keepdims=True)
        gated = acc[:, pl.ds(pl.multiple_of(768 + h * HD, HD), HD)]
        ybuf[:, cols] = (attn * lax.rsqrt(square + 1e-06) * gated).astype(BF)

    pltpu.make_async_remote_copy(
        src_ref=sbf.at[core], dst_ref=spart.at[1 - core], send_sem=sts.at[5], recv_sem=str_.at[5],
        device_id={"seq": partner}, device_id_type=MESH,
    ).wait()
    finish(core, isend)
    back.wait()
    finish(1 - core, ibuf)

    def blk(h, dp, dq):
        return (dq * RING + dp if h == 0 else dp * RING + dq) * ROWS

    def outproj(h, dq):
        if h == 0:
            rows = ybuf[pl.ds(dq * 64, 64), :]
        else:
            rows = jnp.concatenate([ybuf[pl.ds(blk(1, dp, dq), ROWS), :] for dp in range(RING)], axis=0)
        got = jnp.dot(rows, wo[:, pl.ds(h * half, half)], preferred_element_type=F32).astype(BF)
        for dp in range(RING):
            part[h][pl.ds(blk(h, dp, dq), ROWS), :] = got[dp * ROWS:(dp + 1) * ROWS]

    def piece(h, dp, dq, q):
        return part[h].at[pl.ds(blk(h, dp, dq), ROWS), pl.ds(q * quart, quart)]

    def rsend(h, dp, dq, q, n, along, s):
        axis = (prim if along == 0 else sec)[h]
        push(
            piece(h, dp, dq, q), rb.at[h * 30 + n], rss.at[count[1]], rsr.at[h * 30 + n],
            {"tp": near[axis, s]},
        )
        count[1] += 1

    def rwait(h, n):
        pltpu.make_async_remote_copy(
            src_ref=rb.at[h * 30 + n], dst_ref=rb.at[h * 30 + n],
            send_sem=rss.at[0], recv_sem=rsr.at[h * 30 + n],
            device_id={"tp": near["x", 1]}, device_id_type=MESH,
        ).wait_recv()
        return rb[h * 30 + n].astype(F32)

    def n_opp(dp, side):
        return dp * 2 + side

    def n_in(dp, side, q):
        return 8 + dp * 4 + side * 2 + q

    def opposite(h, dp):
        rsend(h, dp, 2, 0, n_opp(dp, 0), 1, 1)
        rsend(h, dp, 2, 1, n_opp(dp, 1), 1, -1)

    def direct(h, dp):
        rsend(h, dp, 1, 1, n_in(dp, 0, 1), 1, 1)
        rsend(h, dp, 3, 0, n_in(dp, 1, 0), 1, -1)

    def merged(h, dp):
        for dq, q, side, s in ((1, 0, 0, 1), (3, 1, 1, -1)):
            got = rwait(h, n_opp(dp, side))
            p = piece(h, dp, dq, q)
            p[...] = (p[...].astype(F32) + got).astype(BF)
            rsend(h, dp, dq, q, n_in(dp, side, q), 1, s)

    def gathered(h, dp, q):
        return (
            piece(h, dp, 0, q)[...].astype(F32)
            + rwait(h, n_in(dp, 0, q)) + rwait(h, n_in(dp, 1, q))
        )

    for h in range(2):
        outproj(h, 2)
        opposite(h, 2)
    for h in range(2):
        opposite(h, 1)
    for h in range(2):
        outproj(h, 1)
        outproj(h, 3)
        direct(h, 2)
    for h in range(2):
        opposite(h, 3)
    for h in range(2):
        outproj(h, 0)
    for h in range(2):
        merged(h, 2)
    for h in range(2):
        direct(h, 1)
        direct(h, 3)
        opposite(h, 0)
    for dp in (1, 3):
        for h in range(2):
            merged(h, dp)
    for h in range(2):
        for q, s in ((0, 1), (1, -1)):
            piece(h, 2, 0, q)[...] = gathered(h, 2, q).astype(BF)
            rsend(h, 2, 0, q, 24 + q, 0, s)
    for h in range(2):
        direct(h, 0)
    for h in range(2):
        merged(h, 0)
    for h in range(2):
        for dp, q, side, s in ((1, 1, 0, 1), (3, 0, 1, -1)):
            piece(h, dp, 0, q)[...] = gathered(h, dp, q).astype(BF)
            rsend(h, dp, 0, q, 26 + side * 2 + q, 0, s)
    for h in range(2):
        for dp, q, side, s in ((1, 0, 0, 1), (3, 1, 1, -1)):
            got = gathered(h, dp, q) + rwait(h, 24 + side)
            piece(h, dp, 0, q)[...] = got.astype(BF)
            rsend(h, dp, 0, q, 26 + side * 2 + q, 0, s)
    for c in sent[:-8]:
        c.wait_send()
    for dz in (1, 2, 3):
        @pl.when(z + dz < RING)
        def _(dz=dz):
            pair(tsend, tbuf.at[dz - 1], dz, zpeer(dz)).wait_send()
    puts = []
    for h in range(2):
        for q in range(2):
            got = gathered(h, 0, q) + rwait(h, 26 + q) + rwait(h, 28 + q)
            cols = pl.ds(h * half + q * quart, quart)
            out[:, cols] = got.astype(BF)
            puts.append(pltpu.make_async_copy(out.at[:, cols], outh.at[:, cols], misc.at[5 + h * 2 + q]))
            puts[-1].start()

    for c in sent[-8:]:
        c.wait_send()
    for c in puts:
        c.wait()


def per_device(tokens, proj_weight, out_weight, head_gain, decay_rate):
    d = tokens.shape[1]
    w2 = proj_weight.reshape(d, 4, 2, HD).transpose(0, 2, 1, 3).reshape(d * 8, HD)
    anyspace = pl.BlockSpec(memory_space=pl.ANY)
    far = pl.BlockSpec(memory_space=pltpu.HBM)
    vmem = pl.BlockSpec(memory_space=pltpu.VMEM)
    dma = pltpu.SemaphoreType.DMA
    v = pltpu.VMEM
    half = d // 2
    scratch = [
        v((BLOCK, half), BF), v((BLOCK, half), BF),
        v((d * 8, HD), BF), v((d, 1024), BF), v((256, d), BF),
        v((BLOCK, 1024), F32),
        v((2, BLOCK, BLOCK), F32), v((2, BLOCK, HD), F32), v((2, BLOCK, HD), F32),
        v((BLOCK, 256), BF), v((BLOCK, 256), BF), v((BLOCK, 256), BF),
        v((BLOCK, 256), F32), v((BLOCK, 256), BF),
        v((BLOCK, half), BF), v((BLOCK, half), BF),
        v((60, ROWS, half // 2), BF),
        v((2, HD, HD), F32), v((2, HD, HD), BF), v((2, HD, HD), BF),
        v((HD, HD), BF), v((3, HD, HD), BF), v((HD, HD), F32),
        v((HD, HD), BF), v((HD, HD), BF),
        v((ROWS, d), BF), v((1, 2 * HD), F32), pltpu.SMEM((2,), F32),
        dma((60,)), dma((60,)), dma((60,)), dma((60,)),
        dma((WCHUNKS,)), dma((9,)), dma((6,)), dma((6,)),
    ]
    return pl.pallas_call(
        fused,
        name="fused_layer",
        out_shape=jax.ShapeDtypeStruct(tokens.shape, BF),
        in_specs=[far] * 5,
        out_specs=anyspace,
        scratch_shapes=scratch,
        compiler_params=pltpu.CompilerParams(
            collective_id=0, has_side_effects=True, vmem_limit_bytes=52 * 1024 * 1024
        ),
    )(*(
        pltpu.with_memory_space_constraint(a, pltpu.HBM)
        for a in (tokens, w2, out_weight, head_gain.reshape(1, -1), decay_rate)
    ))


def solution(mesh):
    return jax.shard_map(
        per_device,
        mesh=mesh,
        in_specs=(P(("seq", "tp"), None), P(None, None, "tp"), P("tp", None), P("tp"), P("tp")),
        out_specs=P(("seq", "tp"), None),
        check_vma=False,
    )
```

```python
import jax
import jax.numpy as jnp
from jax import lax
from jax.experimental import pallas as pl
from jax.experimental.pallas import tpu as pltpu
from jax.sharding import PartitionSpec as P

HD = 128
ROWS = 16
BLOCK = 256
RING = 4
WCHUNKS = 6
SLOT = (2, 0, 1, 3)
BF = jnp.bfloat16
F32 = jnp.float32
MESH = pl.DeviceIdType.MESH


def fused(
    tok, w2h, woh, gainh, rateh, outh,
    xga, xgb, w2, wf, wo, acc, mask, odec, idec, qb, kb, vb, ab, ybuf, pa, pb, rb,
    sloc, sbf, spart, tsend, tbuf, inc, isend, ibuf,
    out, gain, rate, ags, agr, rss, rsr, ws, misc, sts, str_,
):
    d = tok.shape[1]
    half = d // 2
    quart = half // 2
    seq = lax.axis_index("seq")
    tp = lax.axis_index("tp")
    z, core = seq // 2, lax.rem(seq, 2)
    x, y = tp // RING, lax.rem(tp, RING)

    def shift(v, s):
        return lax.rem(v + (s + RING), RING)

    near = {
        ("x", s): shift(x, s) * RING + y for s in (1, -1)
    } | {("y", s): x * RING + shift(y, s) for s in (1, -1)}
    prim, sec = ("x", "y"), ("y", "x")
    xg, part = (xga, xgb), (pa, pb)
    partner = z * 2 + (1 - core)

    def zpeer(dz):
        return lax.rem(z + dz, RING) * 2 + core

    barrier = pltpu.get_barrier_semaphore()
    for where in near.values():
        pl.semaphore_signal(barrier, inc=1, device_id={"tp": where}, device_id_type=MESH)
    for where in (partner, zpeer(1), zpeer(2), zpeer(3)):
        pl.semaphore_signal(barrier, inc=1, device_id={"seq": where}, device_id_type=MESH)

    small = [
        pltpu.make_async_copy(rateh, rate, misc.at[3]),
        pltpu.make_async_copy(gainh, gain, misc.at[4]),
    ]
    for c in small:
        c.start()
    wrows = w2.shape[0] // WCHUNKS
    loads = [
        pltpu.make_async_copy(
            w2h.at[pl.ds(c * wrows, wrows)], w2.at[pl.ds(c * wrows, wrows)], ws.at[c]
        )
        for c in range(WCHUNKS)
    ]
    loads[0].start()
    owns = [
        pltpu.make_async_copy(
            tok.at[:, pl.ds(h * half, half)], xg[h].at[pl.ds(0, ROWS)], misc.at[h]
        )
        for h in range(2)
    ]
    for c in owns:
        c.start()
    pl.semaphore_wait(barrier, 8)

    sent = []

    def push(src, dst, ssem, rsem, where):
        c = pltpu.make_async_remote_copy(
            src_ref=src, dst_ref=dst, send_sem=ssem, recv_sem=rsem,
            device_id=where, device_id_type=MESH,
        )
        c.start()
        sent.append(c)

    def spot(h, dp, dq, q):
        return xg[h].at[pl.ds((dq * RING + dp) * ROWS, ROWS), pl.ds(q * quart, quart)]

    def key(h, dp, dq, q):
        return h * 30 + (dq * RING + dp - 1) * 2 + q

    count = [0, 0]

    def gsend(h, dp, dq, q, along, s):
        if dp == 0 and dq == 0:
            src = tok.at[:, pl.ds(h * half + q * quart, quart)]
        else:
            src = spot(h, dp, dq, q)
        if along == 0:
            ndp, ndq, axis = (dp - s) % RING, dq, prim[h]
        else:
            ndp, ndq, axis = dp, (dq - s) % RING, sec[h]
        push(
            src, spot(h, ndp, ndq, q), ags.at[count[0]], agr.at[key(h, ndp, ndq, q)],
            {"tp": near[axis, s]},
        )
        count[0] += 1

    def gwait(h, dp, dq, q):
        pltpu.make_async_remote_copy(
            src_ref=spot(h, dp, dq, q), dst_ref=spot(h, dp, dq, q),
            send_sem=ags.at[0], recv_sem=agr.at[key(h, dp, dq, q)],
            device_id={"tp": near["x", 1]}, device_id_type=MESH,
        ).wait_recv()

    lead = {1: 0, -1: 1}
    for turn in range(2):
        for h in range(2):
            for s in (1, -1):
                gsend(h, 0, 0, lead[s] if turn == 0 else 1 - lead[s], 0, s)
    for turn in range(2):
        for h in range(2):
            for s in (1, -1):
                gsend(h, 0, 0, lead[s] if turn == 0 else 1 - lead[s], 1, s)
    for c in loads[1:]:
        c.start()
    wocopy = pltpu.make_async_copy(woh, wo, misc.at[2])
    wocopy.start()
    for c in small:
        c.wait()

    def place(dim, shape):
        i = lax.broadcasted_iota(jnp.int32, shape, dim)
        blk = i // ROWS
        dx, dy = blk & 3, blk // RING
        return (
            ((((x + dx) & 3) * RING + ((y + dy) & 3)) * ROWS + (i & (ROWS - 1)))
        ).astype(F32)

    diff = place(0, (BLOCK, BLOCK)) - place(1, (BLOCK, BLOCK))
    pos = place(0, (BLOCK, HD))
    for h in range(2):
        r = rate[h]
        mask[h] = jnp.where(diff >= 0.0, jnp.exp(-r * jnp.maximum(diff, 0.0)), 0.0)
        odec[h] = jnp.exp(-r * (BLOCK - 1.0 - pos))
        idec[h] = jnp.exp(-r * (pos + 1.0))
    acc[...] = jnp.zeros_like(acc)

    def reorder(c):
        loads[c].wait()
        each = wrows // 512

        def body(i, carry):
            for u in range(2):
                n = c * each + i * 2 + u
                v = w2[pl.ds(pl.multiple_of(n * 512, 512), 512), :].astype(F32)
                v = jnp.transpose(v.reshape(64, 8, 128), (1, 0, 2))
                r0 = pl.multiple_of(n * 64, 64)
                for e in range(8):
                    col = SLOT[e % 4] * 256 + (e // 4) * 128
                    wf[pl.ds(r0, 64), pl.ds(col, 128)] = v[e].astype(BF)
            return carry

        lax.fori_loop(0, each // 2, body, 0)

    def project(h, g, n):
        cols = pl.ds(n * 512, 512)
        got = jnp.dot(
            xg[h][pl.ds(g * 128, 128), :], wf[pl.ds(h * half, half), cols],
            preferred_element_type=F32,
        )
        if h == 0:
            acc[pl.ds(g * 128, 128), cols] += got
        else:
            for e in range(2):
                for dp in range(RING):
                    at = (e * RING + dp) * ROWS
                    acc[pl.ds((dp * RING + g * 2 + e) * ROWS, ROWS), cols] += got[at:at + ROWS]

    reorder(0)
    reorder(1)
    for h in range(2):
        for dp, q, s in ((3, 0, 1), (1, 1, -1)):
            gwait(h, dp, 0, q)
            gsend(h, dp, 0, q, 0, s)
            gsend(h, dp, 0, q, 1, 1)
            gsend(h, dp, 0, q, 1, -1)
    reorder(2)
    for h in range(2):
        for dq, q, s in ((3, 0, 1), (1, 1, -1)):
            gwait(h, 0, dq, q)
            gsend(h, 0, dq, q, 1, s)
        for dp, q in ((3, 1), (1, 0)):
            gwait(h, dp, 0, q)
            gsend(h, dp, 0, q, 1, 1)
            gsend(h, dp, 0, q, 1, -1)
    reorder(3)
    for h in range(2):
        for q in range(2):
            gwait(h, 2, 0, q)
            gsend(h, 2, 0, q, 1, 1)
            gsend(h, 2, 0, q, 1, -1)
    reorder(4)
    for dp in (3, 1):
        for h in range(2):
            for dq, q, s in ((3, 0, 1), (1, 1, -1)):
                gwait(h, dp, dq, q)
                gsend(h, dp, dq, q, 1, s)
    reorder(5)
    for h in range(2):
        for dq, q, s in ((3, 0, 1), (1, 1, -1)):
            gwait(h, 2, dq, q)
            gsend(h, 2, dq, q, 1, s)
    for c in owns:
        c.wait()
    for h in range(2):
        for dp in (0, 3, 1, 2):
            gwait(h, dp, 1, 0)
        for n in range(2):
            project(h, 0, n)
    for h in range(2):
        for dp in (0, 3, 1, 2):
            gwait(h, dp, 3, 1)
        for dp in (0, 3, 1, 2):
            for q in range(2):
                gwait(h, dp, 2, q)
        project(h, 1, 0)

    def silu(v):
        return v / (1.0 + jnp.exp(-v))

    kb[...] = silu(acc[:, 0:256]).astype(BF)
    vb[...] = silu(acc[:, 256:512]).astype(BF)
    for h in range(2):
        cols = pl.ds(h * HD, HD)
        ks = (kb[:, cols].astype(F32) * odec[h]).astype(BF)
        st = lax.dot_general(
            ks, vb[:, cols], (((0,), (0,)), ((), ())), preferred_element_type=F32
        )
        sloc[h] = st
        sbf[h] = st.astype(BF)

    def pair(src, dst, n, where):
        return pltpu.make_async_remote_copy(
            src_ref=src, dst_ref=dst, send_sem=sts.at[n], recv_sem=str_.at[n],
            device_id={"seq": where}, device_id_type=MESH,
        )

    swap = pair(sbf.at[1 - core], spart.at[1 - core], 0, partner)
    rest = pair(sbf.at[core], spart.at[core], 5, partner)
    swap.start()
    rest.start()

    def inner(h):
        cols = pl.ds(h * HD, HD)
        sc = lax.dot_general(
            qb[:, cols], kb[:, cols], (((1,), (1,)), ((), ())), preferred_element_type=F32
        )
        wt = (sc * mask[h]).astype(BF)
        ab[:, cols] = jnp.dot(wt, vb[:, cols], preferred_element_type=F32)

    def decay(r, n):
        return jnp.exp(jnp.full((1, HD), -r * n, F32))

    pltpu.make_async_remote_copy(
        src_ref=sbf.at[1 - core], dst_ref=spart.at[core], send_sem=sts.at[0], recv_sem=str_.at[0],
        device_id={"seq": partner}, device_id_type=MESH,
    ).wait()
    mine, other = sloc[core], spart[core].astype(F32)
    fall = decay(rate[core], float(BLOCK))
    first = core == 0
    one = jnp.ones_like(fall)
    chip = jnp.where(first, fall, one) * mine + jnp.where(first, one, fall) * other
    tsend[...] = chip.astype(BF)
    for dz in (1, 2, 3):
        @pl.when(z + dz < RING)
        def _(dz=dz):
            pair(tsend, tbuf.at[dz - 1], dz, zpeer(dz)).start()

    project(0, 1, 1)
    project(1, 1, 1)
    qb[...] = silu(acc[:, 512:768]).astype(BF)
    inner(0)
    inner(1)
    gate = 1.0 / (1.0 + jnp.exp(-acc[:, 768:1024]))
    acc[:, 768:1024] = gate * gain[...]
    inc[...] = jnp.zeros_like(inc)
    for dz in (1, 2, 3):
        @pl.when(z >= dz)
        def _(dz=dz):
            pair(tsend, tbuf.at[dz - 1], dz, zpeer(dz)).wait_recv()
            inc[...] += decay(rate[core], float(2 * BLOCK * (dz - 1))) * tbuf[dz - 1].astype(F32)

    isend[...] = inc[...].astype(BF)
    back = pair(isend, ibuf, 4, partner)
    back.start()
    wocopy.wait()

    def finish(h, into):
        cols = pl.ds(pl.multiple_of(h * HD, HD), HD)
        chipin = into[...].astype(F32)
        fallh = decay(rate[h], float(BLOCK))
        state = jnp.where(first, chipin, fallh * chipin + spart[h].astype(F32))
        carried = jnp.dot(qb[:, cols], state.astype(BF), preferred_element_type=F32)
        attn = ab[:, cols] + carried * idec[h]
        square = jnp.mean(attn * attn, axis=-1, keepdims=True)
        gated = acc[:, pl.ds(pl.multiple_of(768 + h * HD, HD), HD)]
        ybuf[:, cols] = (attn * lax.rsqrt(square + 1e-06) * gated).astype(BF)

    pltpu.make_async_remote_copy(
        src_ref=sbf.at[core], dst_ref=spart.at[1 - core], send_sem=sts.at[5], recv_sem=str_.at[5],
        device_id={"seq": partner}, device_id_type=MESH,
    ).wait()
    finish(core, isend)
    back.wait()
    finish(1 - core, ibuf)

    def blk(h, dp, dq):
        return (dq * RING + dp if h == 0 else dp * RING + dq) * ROWS

    def outproj(h, dq):
        if h == 0:
            rows = ybuf[pl.ds(dq * 64, 64), :]
        else:
            rows = jnp.concatenate([ybuf[pl.ds(blk(1, dp, dq), ROWS), :] for dp in range(RING)], axis=0)
        got = jnp.dot(rows, wo[:, pl.ds(h * half, half)], preferred_element_type=F32).astype(BF)
        for dp in range(RING):
            part[h][pl.ds(blk(h, dp, dq), ROWS), :] = got[dp * ROWS:(dp + 1) * ROWS]

    def piece(h, dp, dq, q):
        return part[h].at[pl.ds(blk(h, dp, dq), ROWS), pl.ds(q * quart, quart)]

    def rsend(h, dp, dq, q, n, along, s):
        axis = (prim if along == 0 else sec)[h]
        push(
            piece(h, dp, dq, q), rb.at[h * 30 + n], rss.at[count[1]], rsr.at[h * 30 + n],
            {"tp": near[axis, s]},
        )
        count[1] += 1

    def rwait(h, n):
        pltpu.make_async_remote_copy(
            src_ref=rb.at[h * 30 + n], dst_ref=rb.at[h * 30 + n],
            send_sem=rss.at[0], recv_sem=rsr.at[h * 30 + n],
            device_id={"tp": near["x", 1]}, device_id_type=MESH,
        ).wait_recv()
        return rb[h * 30 + n].astype(F32)

    def n_opp(dp, side):
        return dp * 2 + side

    def n_in(dp, side, q):
        return 8 + dp * 4 + side * 2 + q

    def opposite(h, dp):
        rsend(h, dp, 2, 0, n_opp(dp, 0), 1, 1)
        rsend(h, dp, 2, 1, n_opp(dp, 1), 1, -1)

    def direct(h, dp):
        rsend(h, dp, 1, 1, n_in(dp, 0, 1), 1, 1)
        rsend(h, dp, 3, 0, n_in(dp, 1, 0), 1, -1)

    def merged(h, dp):
        for dq, q, side, s in ((1, 0, 0, 1), (3, 1, 1, -1)):
            got = rwait(h, n_opp(dp, side))
            p = piece(h, dp, dq, q)
            p[...] = (p[...].astype(F32) + got).astype(BF)
            rsend(h, dp, dq, q, n_in(dp, side, q), 1, s)

    def gathered(h, dp, q):
        return (
            piece(h, dp, 0, q)[...].astype(F32)
            + rwait(h, n_in(dp, 0, q)) + rwait(h, n_in(dp, 1, q))
        )

    for h in range(2):
        outproj(h, 2)
        opposite(h, 2)
    for h in range(2):
        opposite(h, 1)
    for h in range(2):
        outproj(h, 1)
        outproj(h, 3)
        direct(h, 2)
    for h in range(2):
        opposite(h, 3)
    for h in range(2):
        outproj(h, 0)
    for h in range(2):
        merged(h, 2)
    for h in range(2):
        direct(h, 1)
        direct(h, 3)
        opposite(h, 0)
    for dp in (1, 3):
        for h in range(2):
            merged(h, dp)
    for h in range(2):
        for q, s in ((0, 1), (1, -1)):
            piece(h, 2, 0, q)[...] = gathered(h, 2, q).astype(BF)
            rsend(h, 2, 0, q, 24 + q, 0, s)
    for h in range(2):
        direct(h, 0)
    for h in range(2):
        merged(h, 0)
    for h in range(2):
        for dp, q, side, s in ((1, 1, 0, 1), (3, 0, 1, -1)):
            piece(h, dp, 0, q)[...] = gathered(h, dp, q).astype(BF)
            rsend(h, dp, 0, q, 26 + side * 2 + q, 0, s)
    for h in range(2):
        for dp, q, side, s in ((1, 0, 0, 1), (3, 1, 1, -1)):
            got = gathered(h, dp, q) + rwait(h, 24 + side)
            piece(h, dp, 0, q)[...] = got.astype(BF)
            rsend(h, dp, 0, q, 26 + side * 2 + q, 0, s)
    puts = []
    for h in range(2):
        for q in range(2):
            got = gathered(h, 0, q) + rwait(h, 26 + q) + rwait(h, 28 + q)
            cols = pl.ds(h * half + q * quart, quart)
            out[:, cols] = got.astype(BF)
            puts.append(pltpu.make_async_copy(out.at[:, cols], outh.at[:, cols], misc.at[5 + h * 2 + q]))
            puts[-1].start()

    for c in sent:
        c.wait_send()
    for c in puts:
        c.wait()
    for dz in (1, 2, 3):
        @pl.when(z + dz < RING)
        def _(dz=dz):
            pair(tsend, tbuf.at[dz - 1], dz, zpeer(dz)).wait_send()


def per_device(tokens, proj_weight, out_weight, head_gain, decay_rate):
    d = tokens.shape[1]
    w2 = proj_weight.reshape(d, 4, 2, HD).transpose(0, 2, 1, 3).reshape(d * 8, HD)
    anyspace = pl.BlockSpec(memory_space=pl.ANY)
    far = pl.BlockSpec(memory_space=pltpu.HBM)
    vmem = pl.BlockSpec(memory_space=pltpu.VMEM)
    dma = pltpu.SemaphoreType.DMA
    v = pltpu.VMEM
    half = d // 2
    scratch = [
        v((BLOCK, half), BF), v((BLOCK, half), BF),
        v((d * 8, HD), BF), v((d, 1024), BF), v((256, d), BF),
        v((BLOCK, 1024), F32),
        v((2, BLOCK, BLOCK), F32), v((2, BLOCK, HD), F32), v((2, BLOCK, HD), F32),
        v((BLOCK, 256), BF), v((BLOCK, 256), BF), v((BLOCK, 256), BF),
        v((BLOCK, 256), F32), v((BLOCK, 256), BF),
        v((BLOCK, half), BF), v((BLOCK, half), BF),
        v((60, ROWS, half // 2), BF),
        v((2, HD, HD), F32), v((2, HD, HD), BF), v((2, HD, HD), BF),
        v((HD, HD), BF), v((3, HD, HD), BF), v((HD, HD), F32),
        v((HD, HD), BF), v((HD, HD), BF),
        v((ROWS, d), BF), v((1, 2 * HD), F32), pltpu.SMEM((2,), F32),
        dma((60,)), dma((60,)), dma((60,)), dma((60,)),
        dma((WCHUNKS,)), dma((9,)), dma((6,)), dma((6,)),
    ]
    return pl.pallas_call(
        fused,
        name="fused_layer",
        out_shape=jax.ShapeDtypeStruct(tokens.shape, BF),
        in_specs=[far] * 5,
        out_specs=anyspace,
        scratch_shapes=scratch,
        compiler_params=pltpu.CompilerParams(
            collective_id=0, has_side_effects=True, vmem_limit_bytes=52 * 1024 * 1024
        ),
    )(*(
        pltpu.with_memory_space_constraint(a, pltpu.HBM)
        for a in (tokens, w2, out_weight, head_gain.reshape(1, -1), decay_rate)
    ))


def solution(mesh):
    return jax.shard_map(
        per_device,
        mesh=mesh,
        in_specs=(P(("seq", "tp"), None), P(None, None, "tp"), P("tp", None), P("tp"), P("tp")),
        out_specs=P(("seq", "tp"), None),
        check_vma=False,
    )
```
